32 devices in a mesh: req: 8 (over z, x), mlp: 4 (over y, core).
Axes of the slice: x: 2, y: 2, z: 4, core: 2. Of those that a mesh axis runs over, the one named last changes fastest.
Arguments:
- hidden_in: bfloat16 [256, 24, 2048], P('mlp', 'req'), may hold values from -6 to 6
- input_gain: float32 [2048], replicated, may hold values from 0.1 to 1.9
- query_weight: bfloat16 [2048, 2048], P(None, 'mlp'), may hold values from -0.125 to 0.125
- keyval_weight: bfloat16 [2048, 1024], P(None, 'mlp'), may hold values from -0.125 to 0.125
- query_gain: float32 [256], replicated, may hold values from 0.5 to 40
- key_gain: float32 [256], replicated, may hold values from 0.1 to 1.9
- out_weight: bfloat16 [2048, 2048], P('mlp'), may hold values from -0.125 to 0.125
- attn_gain: float32 [2048], replicated, may hold values from 0.1 to 1.9
- laurel_left: bfloat16 [2048, 64], replicated, may hold values from -0.125 to 0.125
- laurel_right: bfloat16 [64, 2048], replicated, may hold values from -0.75 to 0.75
- laurel_gain: float32 [2048], replicated, may hold values from 0.1 to 1.9
- ffn_gain: float32 [2048], replicated, may hold values from 0.1 to 1.9
- post_gain: float32 [2048], replicated, may hold values from 0.1 to 1.9
- gate_projection_matrix: bfloat16 [2048, 4096], P(None, 'mlp'), may hold values from -0.125 to 0.125
- up_projection_matrix: bfloat16 [2048, 4096], P(None, 'mlp'), may hold values from -0.125 to 0.125
- down_projection_matrix: bfloat16 [4096, 2048], P('mlp'), may hold values from -0.09375 to 0.09375
- page_pool: bfloat16 [16, 128, 1024], P('req'), may hold values from -6 to 6
- page_owner: int32 [2, 8], replicated, may hold values from 0 to 7, as said below
- page_slot: int32 [2, 8], replicated, may hold values from 0 to 1
- request_group: int32 [24], P('req'), may hold values from 0 to 1, as said below
- suffix_len: int32 [24], P('req'), may hold values from 64 to 256
Outputs:
- hidden_out: bfloat16 [256, 24, 2048], P('mlp', 'req')
- new_pages: bfloat16 [256, 24, 1024], P(None, 'req', 'mlp')
The draws below stay inside these ranges and needn't reach their ends.
Inputs may be any that keep to these rules, and one draw needn't show every extreme that they name: `request_group`: each group has exactly 12 requests. The pairs (page_owner, page_slot) name every page of the pool exactly once.
All inputs are finite; a program needn't handle non-finite values.
Results may differ from the reference program's by a relative error of at most 0.013.
The reference program's roundings to bfloat16 on the way count: a program that leaves them out, or rounds other values in their place, can miss the bound.
Values may be sent and summed in bfloat16 or wider, within the bound.
No kernel may reach another device: no remote copies, remote signals or barrier semaphores. Data moves between devices by JAX's collectives and lax.ppermute only.
A program may use at most 128 MiB of HBM per device.

```python
import math
import jax
import jax.numpy as jnp
from jax import lax

D = 2048
HEADS = 8
KV_HEADS = 2
HD = 256
RANK = 64
FF = 4096
PAGE = 128
SUF = 256
PREFIX_PAGES = 8
GROUP_REQ = 12
REQUESTS = 24
GROUPS = 2
POOL_DEV = 2
N_REQ = 8
N_MLP = 4


def pool_order(key):
    shuffled = jax.random.permutation(jax.random.fold_in(key, 11), GROUPS * PREFIX_PAGES)
    return shuffled.reshape(GROUPS, PREFIX_PAGES).astype(jnp.int32)


def draw_page_owner(key, part):
    return pool_order(key) // POOL_DEV


def draw_page_slot(key, part):
    return pool_order(key) % POOL_DEV


def draw_request_group(key, part):
    shuffled = jax.random.permutation(jax.random.fold_in(key, 23), REQUESTS)
    return (shuffled // GROUP_REQ).astype(jnp.int32)


def draw_suffix_len(key, part):
    lengths = jax.random.randint(jax.random.fold_in(key, 31), (REQUESTS,), SUF // 4, SUF + 1)
    chosen = jax.random.permutation(jax.random.fold_in(key, 37), REQUESTS)
    lengths = lengths.at[chosen[0]].set(SUF)
    lengths = lengths.at[chosen[1]].set(SUF // 4)
    return lengths.astype(jnp.int32)


def draw_query_gain(key, part):
    return jnp.exp(jax.random.uniform(jax.random.fold_in(key, 41), (HD,), jnp.float32, math.log(0.5), math.log(2.0)))


def shard_levels(stream_key, extent, split, low, high):
    def one(position, parts):
        steps = jax.random.uniform(jax.random.fold_in(jax.random.fold_in(stream_key, 6), position), (parts,), jnp.float32, low / len(split), high / len(split))
        return jnp.repeat(jnp.exp(steps), extent[position] // parts).reshape((-1,) + (1,) * (len(extent) - position - 1))

    gain = one(*split[0])
    for cut in split[1:]:
        gain = gain * one(*cut)
    return gain


def normal_values(rng, dims, scale, most, pieces=(), held_as=jnp.bfloat16):
    array = scale * jax.random.normal(rng, dims, jnp.float32)
    if pieces:
        array = array * shard_levels(rng, dims, pieces, -0.22, 0.18)
    return jnp.clip(array, -most, most).astype(held_as)


def setup_inputs(seed: int = 0) -> dict:
    arg_keys = jax.random.split(jax.random.key(seed), 22)
    hidden_in = normal_values(arg_keys[0], (SUF, REQUESTS, D), 1.0, 6.0, ((0, 4), (1, 8)))
    input_gain = jnp.clip(1.0 + 0.18 * jax.random.normal(arg_keys[1], (D,), jnp.float32), 0.1, 1.9)
    query_weight = normal_values(arg_keys[2], (D, HEADS * HD), D ** -0.5, 0.125, ((1, 4),))
    keyval_weight = normal_values(arg_keys[3], (D, KV_HEADS * 2 * HD), D ** -0.5, 0.125, ((1, 4),))
    query_gain = draw_query_gain(jax.random.fold_in(arg_keys[21], 71), 0)
    key_gain = jnp.clip(1.0 + 0.18 * jax.random.normal(arg_keys[5], (HD,), jnp.float32), 0.1, 1.9)
    out_weight = normal_values(arg_keys[6], (HEADS * HD, D), (HEADS * HD) ** -0.5, 0.125, ((0, 4),))
    attn_gain = jnp.clip(1.0 + 0.18 * jax.random.normal(arg_keys[7], (D,), jnp.float32), 0.1, 1.9)
    laurel_left = normal_values(arg_keys[8], (D, RANK), D ** -0.5, 0.125)
    laurel_right = normal_values(arg_keys[9], (RANK, D), RANK ** -0.5, 0.75)
    laurel_gain = jnp.clip(1.0 + 0.18 * jax.random.normal(arg_keys[10], (D,), jnp.float32), 0.1, 1.9)
    ffn_gain = jnp.clip(1.0 + 0.18 * jax.random.normal(arg_keys[11], (D,), jnp.float32), 0.1, 1.9)
    post_gain = jnp.clip(1.0 + 0.18 * jax.random.normal(arg_keys[12], (D,), jnp.float32), 0.1, 1.9)
    gate_projection_matrix = normal_values(arg_keys[13], (D, FF), D ** -0.5, 0.125, ((1, 4),))
    up_projection_matrix = normal_values(arg_keys[14], (D, FF), D ** -0.5, 0.125, ((1, 4),))
    down_projection_matrix = normal_values(arg_keys[15], (FF, D), FF ** -0.5, 0.09375, ((0, 4),))
    page_pool = normal_values(arg_keys[16], (N_REQ * POOL_DEV, PAGE, KV_HEADS * 2 * HD), 1.0, 6.0, ((0, 8),))
    page_owner = draw_page_owner(jax.random.fold_in(arg_keys[21], 71), 0)
    page_slot = draw_page_slot(jax.random.fold_in(arg_keys[21], 71), 0)
    request_group = draw_request_group(jax.random.fold_in(arg_keys[21], 71), 0)
    suffix_len = draw_suffix_len(jax.random.fold_in(arg_keys[21], 71), 0)
    return {"hidden_in": hidden_in, "input_gain": input_gain, "query_weight": query_weight, "keyval_weight": keyval_weight, "query_gain": query_gain, "key_gain": key_gain, "out_weight": out_weight, "attn_gain": attn_gain, "laurel_left": laurel_left, "laurel_right": laurel_right, "laurel_gain": laurel_gain, "ffn_gain": ffn_gain, "post_gain": post_gain, "gate_projection_matrix": gate_projection_matrix, "up_projection_matrix": up_projection_matrix, "down_projection_matrix": down_projection_matrix, "page_pool": page_pool, "page_owner": page_owner, "page_slot": page_slot, "request_group": request_group, "suffix_len": suffix_len}


EPS = 1e-06
INV_ROOT = 1.0 / math.sqrt(2.0)

def rms_norm(values, norm_gain):
    values = values.astype(jnp.float32)
    return values * lax.rsqrt(lax.optimization_barrier(jnp.mean(values * values, axis=-1, keepdims=True)) + EPS) * norm_gain

def rotary(values, first_row):
    row_count = values.shape[0]
    halfway = values.shape[-1] // 2
    frequency = 1000000.0 ** (-jnp.arange(halfway, dtype=jnp.float32) / halfway)
    positions = (first_row + jnp.arange(row_count)).astype(jnp.float32)
    angles = positions[:, None] * frequency[None, :]
    cos_table = jnp.cos(angles)[:, None, None, :]
    sin_table = jnp.sin(angles)[:, None, None, :]
    first_half = values[..., :halfway]
    second_half = values[..., halfway:]
    return jnp.concatenate([first_half * cos_table - second_half * sin_table, second_half * cos_table + first_half * sin_table], axis=-1)

def reference(hidden_in, input_gain, query_weight, keyval_weight, query_gain, key_gain, out_weight, attn_gain, laurel_left, laurel_right, laurel_gain, ffn_gain, post_gain, gate_projection_matrix, up_projection_matrix, down_projection_matrix, page_pool, page_owner, page_slot, request_group, suffix_len):
    prefix_len = PREFIX_PAGES * PAGE
    kv_groups = HEADS // KV_HEADS
    total_rows = SUF * REQUESTS
    active = rms_norm(hidden_in, input_gain).astype(jnp.bfloat16)
    flat_active = active.reshape(total_rows, D)
    queries = jnp.dot(flat_active, query_weight, preferred_element_type=jnp.float32).reshape(SUF, REQUESTS, HEADS, HD)
    queries = lax.optimization_barrier(rotary(rms_norm(queries, query_gain), prefix_len).astype(jnp.bfloat16))
    keyval = jnp.dot(flat_active, keyval_weight, preferred_element_type=jnp.float32).reshape(SUF, REQUESTS, KV_HEADS, 2, HD)
    keys_new = rotary(rms_norm(keyval[:, :, :, 0], key_gain), prefix_len)
    values_new = rms_norm(keyval[:, :, :, 1], 1.0)
    live = jnp.arange(SUF)[:, None] < suffix_len[None, :]
    stacked = jnp.stack([keys_new, values_new], axis=3)
    new_pages = lax.optimization_barrier(jnp.where(live[:, :, None, None, None], stacked, 0.0).astype(jnp.bfloat16))
    page_ids = page_owner * POOL_DEV + page_slot
    causal = jnp.arange(SUF)[None, :] <= jnp.arange(SUF)[:, None]

    def attend(req_index):
        group_id = request_group[req_index]
        pages = jnp.take(page_pool, page_ids[group_id], axis=0).reshape(prefix_len, KV_HEADS, 2, HD)
        own_kv = new_pages[:, req_index]
        joined = jnp.concatenate([pages, own_kv], axis=0).astype(jnp.float32)
        query_rows = queries[:, req_index].reshape(SUF, KV_HEADS, kv_groups, HD).astype(jnp.float32)
        scores = jnp.einsum('tkgd,skd->kgts', query_rows, joined[:, :, 0]) * HD ** (-0.5)
        live_count = suffix_len[req_index]
        suffix_ok = causal & (jnp.arange(SUF)[None, :] < live_count)
        allowed = jnp.concatenate([jnp.ones((SUF, prefix_len), dtype=bool), suffix_ok], axis=1)
        scores = jnp.where(allowed, scores, -jnp.inf)
        row_peak = lax.optimization_barrier(jnp.max(scores, axis=-1, keepdims=True))
        exp_terms = jnp.exp(scores - row_peak)
        totals = lax.optimization_barrier(jnp.sum(exp_terms, axis=-1))
        weights = lax.optimization_barrier(exp_terms.astype(jnp.bfloat16)).astype(jnp.float32)
        mixed_rows = jnp.einsum('kgts,skd->tkgd', weights, joined[:, :, 1])
        mixed_rows = mixed_rows / jnp.transpose(totals, (2, 0, 1))[..., None]
        return mixed_rows.reshape(SUF, HEADS * HD).astype(jnp.bfloat16)
    attended = lax.map(attend, jnp.arange(REQUESTS))
    flat_attended = jnp.transpose(attended, (1, 0, 2)).reshape(total_rows, HEADS * HD)
    slice_cols = HEADS * HD // N_MLP
    attn_summed = jnp.zeros((total_rows, D), jnp.float32)
    for member in range(N_MLP):
        lower_col = member * slice_cols
        partial_term = jnp.dot(flat_attended[:, lower_col:lower_col + slice_cols], out_weight[lower_col:lower_col + slice_cols], preferred_element_type=jnp.float32)
        attn_summed = attn_summed + lax.optimization_barrier(partial_term.astype(jnp.bfloat16)).astype(jnp.float32)
    attn_summed = attn_summed.reshape(SUF, REQUESTS, D)
    laurel_mid = jnp.dot(flat_active, laurel_left, preferred_element_type=jnp.float32).astype(jnp.bfloat16)
    laurel_out = active.astype(jnp.float32) + rms_norm(jnp.dot(laurel_mid, laurel_right, preferred_element_type=jnp.float32).reshape(SUF, REQUESTS, D), laurel_gain)
    residual = (hidden_in.astype(jnp.float32) + rms_norm(attn_summed, attn_gain) + laurel_out) * INV_ROOT
    ffn_in = rms_norm(residual, ffn_gain).astype(jnp.bfloat16).reshape(total_rows, D)
    slice_units = FF // N_MLP
    ffn_summed = jnp.zeros((total_rows, D), jnp.float32)
    for member in range(N_MLP):
        lower_unit = member * slice_units
        gate_portion = jnp.dot(ffn_in, gate_projection_matrix[:, lower_unit:lower_unit + slice_units], preferred_element_type=jnp.float32)
        up_portion = jnp.dot(ffn_in, up_projection_matrix[:, lower_unit:lower_unit + slice_units], preferred_element_type=jnp.float32)
        expanded = (jax.nn.gelu(gate_portion, approximate=True) * up_portion).astype(jnp.bfloat16)
        partial_term = jnp.dot(expanded, down_projection_matrix[lower_unit:lower_unit + slice_units], preferred_element_type=jnp.float32)
        ffn_summed = ffn_summed + lax.optimization_barrier(partial_term.astype(jnp.bfloat16)).astype(jnp.float32)
    output = residual + rms_norm(ffn_summed.reshape(SUF, REQUESTS, D), post_gain)
    hidden_out = jnp.where(live[:, :, None], output, 0.0).astype(jnp.bfloat16)
    return (hidden_out, new_pages.reshape(SUF, REQUESTS, KV_HEADS * 2 * HD))
```

```python
import functools
import math

import jax
import jax.numpy as jnp
from jax import lax
from jax.experimental import pallas as pl
from jax.experimental.pallas import tpu as pltpu
from jax.sharding import PartitionSpec as P

EPS = 1e-06
INV_ROOT = 1.0 / math.sqrt(2.0)
BF16 = jnp.bfloat16
F32 = jnp.float32
ON_CHIP = pl.BlockSpec(memory_space=pltpu.VMEM)
SCALARS = pl.BlockSpec(memory_space=pltpu.SMEM)
ANYWHERE = pl.BlockSpec(memory_space=pl.ANY)
BLOCK_XOR = (0, 2, 1, 3)


def exchange(value, axis, flip):
    return lax.ppermute(value, axis, [(i, i ^ flip) for i in range(lax.axis_size(axis))])


def normed(values, gain):
    scale = lax.rsqrt(jnp.mean(values * values, axis=-1, keepdims=True) + EPS)
    return values * scale * gain


def rotated(values, cos, sin):
    half = values.shape[-1] // 2
    first, second = values[:, :half], values[:, half:]
    return jnp.concatenate(
        [first * cos - second * sin, second * cos + first * sin], axis=-1
    )


def params(mib):
    return pltpu.CompilerParams(vmem_limit_bytes=mib << 20)


def cost(flops, moved, exps=0):
    return pl.CostEstimate(flops=int(flops), bytes_accessed=int(moved), transcendentals=int(exps))


def active_kernel(hidden_ref, gain_ref, *active_refs):
    for r, active_ref in enumerate(active_refs):
        active_ref[...] = normed(hidden_ref[r].astype(F32), gain_ref[...]).astype(BF16)


def make_active(hidden, gain):
    reqs, rows, width = hidden.shape
    return pl.pallas_call(
        active_kernel,
        out_shape=[jax.ShapeDtypeStruct((rows, width), BF16)] * reqs,
        in_specs=[ON_CHIP, ON_CHIP],
        out_specs=[ON_CHIP] * reqs,
        cost_estimate=cost(6 * hidden.size, 4 * hidden.size),
        name="active",
    )(hidden, gain)


def base_kernel(hidden_ref, *refs):
    reqs = hidden_ref.shape[0]
    active_refs = refs[:reqs]
    left_ref, right_ref, gain_ref = refs[reqs : reqs + 3]
    base_refs = refs[reqs + 3 :]
    for r in range(reqs):
        active = active_refs[r][...]
        mid = lax.dot_general(
            active, left_ref[...], (((1,), (1,)), ((), ())), preferred_element_type=F32
        ).astype(BF16)
        low = jnp.dot(mid, right_ref[...], preferred_element_type=F32)
        base_refs[r][...] = (
            hidden_ref[r].astype(F32) + active.astype(F32) + normed(low, gain_ref[...])
        )


def make_base(hidden, actives, left_t, right, gain):
    reqs, rows, width = hidden.shape
    return pl.pallas_call(
        base_kernel,
        out_shape=[jax.ShapeDtypeStruct((rows, width), F32)] * reqs,
        in_specs=[ON_CHIP] * (reqs + 4),
        out_specs=[ON_CHIP] * reqs,
        cost_estimate=cost(4 * hidden.size * left_t.shape[0], 8 * hidden.size),
        name="base",
    )(hidden, *actives, left_t, right, gain)


def project_kernel(
    req,
    len_ref,
    own_ref,
    y_ref,
    c_ref,
    d_ref,
    wq_ref,
    mine_ref,
    other_ref,
    qgain_ref,
    kgain_ref,
    cos_ref,
    sin_ref,
    *refs,
):
    page_ref, q_ref, k_ref, v_ref = refs[-4:]
    member = lax.axis_index("mlp")
    part = own_ref.shape[0]
    head = qgain_ref.shape[-1]
    rows = jnp.concatenate([own_ref[...], y_ref[...], c_ref[...], d_ref[...]], axis=0)
    starts = [pl.multiple_of((member ^ flip) * part, part) for flip in BLOCK_XOR]
    cos = jnp.concatenate([cos_ref[pl.ds(s, part), :] for s in starts], axis=0)
    sin = jnp.concatenate([sin_ref[pl.ds(s, part), :] for s in starts], axis=0)
    count = rows.shape[0]
    mine = jnp.dot(rows, mine_ref[...], preferred_element_type=F32)
    other = jnp.dot(rows, other_ref[...], preferred_element_type=F32)
    holds_keys = member % 2 == 0
    raw_keys = jnp.where(holds_keys, mine, other)
    raw_values = jnp.where(holds_keys, other, mine)
    keys = rotated(normed(raw_keys, kgain_ref[...]), cos, sin).astype(BF16)
    values = normed(raw_values, 1.0).astype(BF16)
    k_ref[...] = keys
    v_ref[...] = values
    live = len_ref[req]
    for b, start in enumerate(starts):
        block = slice(b * part, (b + 1) * part)
        piece = jnp.where(
            holds_keys, keys[block].astype(F32), values[block].astype(F32)
        )
        position = start + lax.broadcasted_iota(jnp.int32, (part, 1), 0)
        page_ref[0, pl.ds(start, part), :] = jnp.where(position < live, piece, 0.0).astype(BF16)
    heads = wq_ref.shape[1] // head
    for h in range(heads):
        raw = jnp.dot(rows, wq_ref[:, h * head : (h + 1) * head], preferred_element_type=F32)
        q_ref[h * count : (h + 1) * count, :] = rotated(
            normed(raw, qgain_ref[...]), cos, sin
        ).astype(BF16)


def project(req, reqs, lens, blocks, wq, mine, other, qgain, kgain, cos, sin, pages):
    part, width = blocks[0].shape
    count = part * len(blocks)
    head = qgain.shape[-1]
    heads = wq.shape[1] // head
    extra = [] if pages is None else [pages]
    return pl.pallas_call(
        functools.partial(project_kernel, req),
        grid=(1,),
        out_shape=[
            jax.ShapeDtypeStruct((reqs, count, head), BF16),
            jax.ShapeDtypeStruct((heads * count, head), BF16),
            jax.ShapeDtypeStruct((count, head), BF16),
            jax.ShapeDtypeStruct((count, head), BF16),
        ],
        in_specs=[SCALARS] + [ON_CHIP] * 11 + [ANYWHERE] * len(extra),
        out_specs=[
            pl.BlockSpec((1, count, head), lambda i: (req, 0, 0)),
            ON_CHIP,
            ON_CHIP,
            ON_CHIP,
        ],
        input_output_aliases={12: 0} if extra else {},
        compiler_params=params(24),
        cost_estimate=cost(2 * count * width * (heads + 2) * head, 6 << 20),
        name="project",
    )(lens, *blocks, wq, mine, other, qgain, kgain, cos, sin, *extra)


def attend_kernel(
    req,
    sources,
    group_ref,
    owner_ref,
    slot_ref,
    q_ref,
    k_ref,
    v_ref,
    wo_ref,
    *refs,
):
    pool_count = len({name for name, _, _, _ in sources})
    pool_refs = refs[:pool_count]
    own_out, y_out, c_out, d_out = refs[pool_count : pool_count + 4]
    prefix, mixed, place, sems = refs[pool_count + 4 :]
    member = lax.axis_index("mlp")
    me = lax.axis_index("req")
    head = k_ref.shape[1]
    count = k_ref.shape[0]
    part = count // 4
    page = pool_refs[0].shape[1]
    n_pages = owner_ref.shape[1]
    per_part = len(sources) // 2
    group = group_ref[req]
    for s in range(len(sources)):
        place[s] = -1
    for i in range(n_pages):
        flip = owner_ref[group, i] ^ me
        far = slot_ref[group, i] ^ (member % 2)
        place[far * per_part + flip] = i
    for name, index, far, flip in sources:
        where = place[far * per_part + flip]

        @pl.when(where >= 0)
        def _():
            start = pl.multiple_of(where * page, page)
            pltpu.make_async_copy(
                pool_refs[name].at[index], prefix.at[pl.ds(start, page), :], sems.at[where]
            ).start()

    for i in range(n_pages):
        pltpu.make_async_copy(
            pool_refs[0].at[0], prefix.at[i * page : (i + 1) * page, :], sems.at[i]
        ).wait()

    factor = head**-0.5 * math.log2(math.e)
    pre = n_pages * page

    def positions(index):
        block = index // part
        flip = (block & 1) * 2 + (block >> 1)
        return (member ^ flip) * part + index % part

    key_at = positions(lax.broadcasted_iota(jnp.int32, (1, count), 1))
    tile = 2 * part
    heads = q_ref.shape[0] // count
    for h in range(heads):
        for first in range(0, count, tile):
            query_at = positions(first + lax.broadcasted_iota(jnp.int32, (tile, 1), 0))
            start = h * count + first
            q = q_ref[start : start + tile, :]
            contract = (((1,), (1,)), ((), ()))
            before = lax.dot_general(
                q, prefix[:, :head], contract, preferred_element_type=F32
            )
            own = lax.dot_general(q, k_ref[...], contract, preferred_element_type=F32)
            own = jnp.where(key_at <= query_at, own, -jnp.inf)
            peak = jnp.maximum(
                jnp.max(before, axis=-1, keepdims=True), jnp.max(own, axis=-1, keepdims=True)
            )
            before = jnp.exp2((before - peak) * factor)
            own = jnp.exp2((own - peak) * factor)
            total = jnp.sum(before, axis=-1, keepdims=True) + jnp.sum(own, axis=-1, keepdims=True)
            out = jnp.dot(before.astype(BF16), prefix[:, head:], preferred_element_type=F32)
            out += jnp.dot(own.astype(BF16), v_ref[...], preferred_element_type=F32)
            mixed[first : first + tile, h * head : (h + 1) * head] = (
                out * (1.0 / total)
            ).astype(BF16)
    width = wo_ref.shape[1]
    step = 512
    for col in range(0, width, step):
        result = jnp.dot(
            mixed[...], wo_ref[:, col : col + step], preferred_element_type=F32
        ).astype(BF16)
        for b, out_ref in enumerate((own_out, y_out, c_out, d_out)):
            out_ref[:, col : col + step] = result[b * part : (b + 1) * part]


def attend(req, sources, group, owner, slot, q, k, v, wo, pools):
    count, head = k.shape
    part = count // 4
    heads = q.shape[0] // count
    page = pools[0].shape[1]
    n_pages = owner.shape[1]
    keys = n_pages * page + count
    return pl.pallas_call(
        functools.partial(attend_kernel, req, sources),
        out_shape=[jax.ShapeDtypeStruct((part, wo.shape[1]), BF16)] * 4,
        in_specs=[SCALARS] * 3 + [ON_CHIP] * 4 + [ANYWHERE] * len(pools),
        out_specs=[ON_CHIP] * 4,
        scratch_shapes=[
            pltpu.VMEM((n_pages * page, 2 * head), BF16),
            pltpu.VMEM((count, heads * head), BF16),
            pltpu.SMEM((len(sources),), jnp.int32),
            pltpu.SemaphoreType.DMA((n_pages,)),
        ],
        compiler_params=params(24),
        cost_estimate=cost(
            heads * count * head * (4 * keys + 2 * wo.shape[1]), 4 << 20, heads * count * keys
        ),
        name="attend",
    )(group, owner, slot, q, k, v, wo, *pools)


def residual_kernel(base_ref, own_ref, c_ref, y_ref, again_ref, fgain_ref, res_ref, in_ref):
    total = own_ref[...].astype(F32) + c_ref[...].astype(F32) + y_ref[...].astype(F32)
    residual = (base_ref[...] + normed(total, again_ref[...])) * INV_ROOT
    res_ref[...] = residual
    in_ref[...] = normed(residual, fgain_ref[...]).astype(BF16)


def make_residual(base, own, c, y, again, fgain):
    return pl.pallas_call(
        residual_kernel,
        out_shape=[
            jax.ShapeDtypeStruct(base.shape, F32),
            jax.ShapeDtypeStruct(base.shape, BF16),
        ],
        in_specs=[ON_CHIP] * 6,
        out_specs=[ON_CHIP] * 2,
        cost_estimate=cost(12 * base.size, 16 * base.size),
        name="residual",
    )(base, own, c, y, again, fgain)


def feed_kernel(own_ref, y_ref, c_ref, d_ref, gate_ref, up_ref, down_ref, *refs):
    outs, hidden = refs[:4], refs[4]
    rows = jnp.concatenate([own_ref[...], y_ref[...], c_ref[...], d_ref[...]], axis=0)
    part = own_ref.shape[0]
    units = gate_ref.shape[1]
    step = 512
    for u in range(0, units, step):
        gate = jnp.dot(rows, gate_ref[:, u : u + step], preferred_element_type=F32)
        up = jnp.dot(rows, up_ref[:, u : u + step], preferred_element_type=F32)
        hidden[:, u : u + step] = (jax.nn.gelu(gate, approximate=True) * up).astype(BF16)
    for col in range(0, down_ref.shape[1], step):
        result = jnp.dot(
            hidden[...], down_ref[:, col : col + step], preferred_element_type=F32
        ).astype(BF16)
        for b, out_ref in enumerate(outs):
            out_ref[:, col : col + step] = result[b * part : (b + 1) * part]


def feed(blocks, gate, up, down):
    part, width = blocks[0].shape
    count = 4 * part
    units = gate.shape[1]
    return pl.pallas_call(
        feed_kernel,
        out_shape=[jax.ShapeDtypeStruct((part, width), BF16)] * 4,
        in_specs=[ON_CHIP] * 7,
        out_specs=[ON_CHIP] * 4,
        scratch_shapes=[pltpu.VMEM((count, units), BF16)],
        compiler_params=params(32),
        cost_estimate=cost(6 * count * width * units, 12 << 20, count * units),
        name="feed",
    )(*blocks, gate, up, down)


def finish_kernel(req, len_ref, res_ref, own_ref, c_ref, y_ref, gain_ref, *refs):
    out_ref = refs[-1]
    part = res_ref.shape[0]
    total = own_ref[...].astype(F32) + c_ref[...].astype(F32) + y_ref[...].astype(F32)
    output = res_ref[...] + normed(total, gain_ref[...])
    position = lax.axis_index("mlp") * part + lax.broadcasted_iota(jnp.int32, (part, 1), 0)
    out_ref[0] = jnp.where(position < len_ref[req], output, 0.0).astype(BF16)


def finish(req, reqs, lens, residual, own, c, y, gain, before):
    part, width = residual.shape
    extra = [] if before is None else [before]
    return pl.pallas_call(
        functools.partial(finish_kernel, req),
        grid=(1,),
        out_shape=jax.ShapeDtypeStruct((reqs, part, width), BF16),
        in_specs=[SCALARS] + [ON_CHIP] * 5 + [ANYWHERE] * len(extra),
        out_specs=pl.BlockSpec((1, part, width), lambda i: (req, 0, 0)),
        input_output_aliases={6: 0} if extra else {},
        cost_estimate=cost(10 * residual.size, 12 * residual.size),
        name="finish",
    )(lens, residual, own, c, y, gain, *extra)


def gather_pool(page_pool, member, width):
    n_req = lax.axis_size("req")
    page = page_pool.shape[1]
    own = lax.dynamic_slice(page_pool, (member % 2, 0, member // 2 * width), (1, page, width))
    direct = {0: own}
    for flip in range(2, n_req, 2):
        direct[flip] = exchange(own, "req", flip)
    direct[1] = exchange(own, "req", 1)
    direct[3] = exchange(direct[2], "req", 1)
    later = list(range(4, n_req, 2))
    arrays = [
        (jnp.concatenate([own, direct[1], direct[2]]), [0, 1, 2]),
        (jnp.concatenate([direct[f] for f in later]), later),
    ]
    crossed = exchange(arrays[1][0], "req", 1)
    arrays.append(
        (jnp.concatenate([direct[3], crossed]), [3] + [f + 1 for f in later])
    )
    pools, sources = [], []
    for far in (0, 1):
        for array, flips in arrays:
            for index, flip in enumerate(flips):
                sources.append((len(pools), index, far, flip))
            pools.append(exchange(array, "mlp", 1) if far else array)
    return pools, sources


def local(
    hidden_in,
    input_gain,
    query_weight,
    keyval_weight,
    query_gain,
    key_gain,
    out_weight,
    attn_gain,
    laurel_left,
    laurel_right,
    laurel_gain,
    ffn_gain,
    post_gain,
    gate_projection_matrix,
    up_projection_matrix,
    down_projection_matrix,
    page_pool,
    page_owner,
    page_slot,
    request_group,
    suffix_len,
):
    member = lax.axis_index("mlp")
    part, reqs, width = hidden_in.shape
    head = query_gain.shape[0]
    count = part * lax.axis_size("mlp")
    prefix_len = page_owner.shape[1] * page_pool.shape[1]
    row = lambda gain: gain[None, :]

    pools, sources = gather_pool(page_pool, member, 2 * head)

    half = head // 2
    frequency = 1000000.0 ** (-jnp.arange(half, dtype=F32) / half)
    angles = (prefix_len + jnp.arange(count)).astype(F32)[:, None] * frequency[None, :]
    cos, sin = jnp.cos(angles), jnp.sin(angles)

    hidden = jnp.transpose(hidden_in, (1, 0, 2))
    actives = make_active(hidden, row(input_gain))
    other_weight = exchange(keyval_weight, "mlp", 1)
    bases = make_base(
        hidden, actives, laurel_left.T, laurel_right, row(laurel_gain)
    )

    def gather(block):
        y = exchange(block, "mlp", 2)
        return [block, y, exchange(block, "mlp", 1), exchange(y, "mlp", 1)]

    def scatter(partials):
        own, y, c, d = partials
        from_c = exchange(d, "mlp", 1)
        joined = (y.astype(F32) + from_c.astype(F32)).astype(BF16)
        return own, exchange(c, "mlp", 1), exchange(joined, "mlp", 2)

    pages = None
    projected = []
    for r in range(reqs):
        pages, q, k, v = project(
            r,
            reqs,
            suffix_len,
            gather(actives[r]),
            query_weight,
            keyval_weight,
            other_weight,
            row(query_gain),
            row(key_gain),
            cos,
            sin,
            pages,
        )
        projected.append((q, k, v))
    residuals = []
    inputs = []
    for r in range(reqs):
        partials = attend(
            r, sources, request_group, page_owner, page_slot, *projected[r], out_weight, pools
        )
        residual, ffn_in = make_residual(
            bases[r], *scatter(partials), row(attn_gain), row(ffn_gain)
        )
        residuals.append(residual)
        inputs.append(gather(ffn_in))
    result = None
    for r in range(reqs):
        partials = feed(
            inputs[r], gate_projection_matrix, up_projection_matrix, down_projection_matrix
        )
        result = finish(
            r, reqs, suffix_len, residuals[r], *scatter(partials), row(post_gain), result
        )
    return jnp.transpose(result, (1, 0, 2)), jnp.transpose(pages, (1, 0, 2))


def solution(mesh):
    placed = (
        P("mlp", "req", None),
        P(),
        P(None, "mlp"),
        P(None, "mlp"),
        P(),
        P(),
        P("mlp", None),
        P(),
        P(),
        P(),
        P(),
        P(),
        P(),
        P(None, "mlp"),
        P(None, "mlp"),
        P("mlp", None),
        P("req", None, None),
        P(),
        P(),
        P("req"),
        P("req"),
    )
    return jax.shard_map(
        local,
        mesh=mesh,
        in_specs=placed,
        out_specs=(P("mlp", "req", None), P(None, "req", "mlp")),
        check_vma=False,
    )
```

```python
import functools
import math

import jax
import jax.numpy as jnp
from jax import lax
from jax.experimental import pallas as pl
from jax.experimental.pallas import tpu as pltpu
from jax.sharding import PartitionSpec as P

EPS = 1e-06
INV_ROOT = 1.0 / math.sqrt(2.0)
BF16 = jnp.bfloat16
F32 = jnp.float32
ON_CHIP = pl.BlockSpec(memory_space=pltpu.VMEM)
SCALARS = pl.BlockSpec(memory_space=pltpu.SMEM)
ANYWHERE = pl.BlockSpec(memory_space=pl.ANY)
BLOCK_XOR = (0, 2, 1, 3)
SPLIT = 2
TILE = 256


def exchange(value, axis, flip):
    return lax.ppermute(value, axis, [(i, i ^ flip) for i in range(lax.axis_size(axis))])


def after(value, *earlier):
    return lax.optimization_barrier((value, *earlier))[0]


def normed(values, gain):
    scale = lax.rsqrt(jnp.mean(values * values, axis=-1, keepdims=True) + EPS)
    return values * scale * gain


def rotated(values, cos, sin):
    half = values.shape[-1] // 2
    first, second = values[:, :half], values[:, half:]
    return jnp.concatenate(
        [first * cos - second * sin, second * cos + first * sin], axis=-1
    )


def params(mib):
    return pltpu.CompilerParams(vmem_limit_bytes=mib << 20)


def cost(flops, moved, exps=0):
    return pl.CostEstimate(flops=1, bytes_accessed=1, transcendentals=0)


def active_rows(hidden, gain):
    return normed(hidden.astype(F32), gain).astype(BF16)


def base_kernel(hidden_ref, gains_ref, left_ref, right_ref, out_ref):
    for r in range(hidden_ref.shape[0]):
        hidden = hidden_ref[r]
        active = active_rows(hidden, gains_ref[0:1, :])
        mid = lax.dot_general(
            active, left_ref[...], (((1,), (1,)), ((), ())), preferred_element_type=F32
        ).astype(BF16)
        low = jnp.dot(mid, right_ref[...], preferred_element_type=F32)
        out_ref[r] = hidden.astype(F32) + active.astype(F32) + normed(low, gains_ref[1:2, :])


def make_base(hidden, gains, left_t, right):
    return pl.pallas_call(
        base_kernel,
        out_shape=jax.ShapeDtypeStruct(hidden.shape, F32),
        in_specs=[ON_CHIP] * 4,
        out_specs=ON_CHIP,
        cost_estimate=cost(4 * hidden.size * left_t.shape[0], 8 * hidden.size),
        compiler_params=params(8),
        name="base",
    )(hidden, gains, left_t, right)


def project_kernel(
    len_ref,
    hidden_ref,
    y_ref,
    c_ref,
    d_ref,
    gains_ref,
    wq_ref,
    mine_ref,
    other_ref,
    head_gains_ref,
    cos_ref,
    sin_ref,
    page_ref,
    q_ref,
    kv_ref,
):
    member = lax.axis_index("mlp")
    reqs, part, _ = hidden_ref.shape
    head = head_gains_ref.shape[-1]
    qgain, kgain = head_gains_ref[0:1, :], head_gains_ref[1:2, :]
    starts = [pl.multiple_of((member ^ flip) * part, part) for flip in BLOCK_XOR]
    cos = jnp.concatenate([cos_ref[pl.ds(s, part), :] for s in starts], axis=0)
    sin = jnp.concatenate([sin_ref[pl.ds(s, part), :] for s in starts], axis=0)
    holds_keys = member % 2 == 0
    heads = wq_ref.shape[1] // head
    for r in range(reqs):
        rows = jnp.concatenate(
            [
                active_rows(ref[r], gains_ref[0:1, :])
                for ref in (hidden_ref, y_ref, c_ref, d_ref)
            ],
            axis=0,
        )
        count = rows.shape[0]
        mine = jnp.dot(rows, mine_ref[...], preferred_element_type=F32)
        other = jnp.dot(rows, other_ref[...], preferred_element_type=F32)
        keys = rotated(normed(jnp.where(holds_keys, mine, other), kgain), cos, sin)
        values = normed(jnp.where(holds_keys, other, mine), 1.0)
        kv_ref[r, :, :head] = keys.astype(BF16)
        kv_ref[r, :, head:] = values.astype(BF16)
        quarter = jnp.where(holds_keys, keys, values)
        live = len_ref[r]
        for b, start in enumerate(starts):
            position = start + lax.broadcasted_iota(jnp.int32, (part, 1), 0)
            page_ref[r, pl.ds(start, part), :] = jnp.where(
                position < live, quarter[b * part : (b + 1) * part], 0.0
            ).astype(BF16)
        for h in range(heads):
            raw = jnp.dot(
                rows, wq_ref[:, h * head : (h + 1) * head], preferred_element_type=F32
            )
            q_ref[r, h * count : (h + 1) * count, :] = rotated(
                normed(raw, qgain), cos, sin
            ).astype(BF16)


def project(lens, hidden, y, c, d, gains, wq, mine, other, head_gains, cos, sin):
    reqs, part, width = hidden.shape
    count = part * len(BLOCK_XOR)
    head = head_gains.shape[-1]
    heads = wq.shape[1] // head
    return pl.pallas_call(
        project_kernel,
        out_shape=[
            jax.ShapeDtypeStruct((reqs, count, head), BF16),
            jax.ShapeDtypeStruct((reqs, heads * count, head), BF16),
            jax.ShapeDtypeStruct((reqs, count, 2 * head), BF16),
        ],
        in_specs=[SCALARS] + [ON_CHIP] * 11,
        out_specs=[ON_CHIP] * 3,
        compiler_params=params(10),
        cost_estimate=cost(2 * reqs * count * width * (heads + 2) * head, 6 << 20),
        name="project",
    )(lens, hidden, y, c, d, gains, wq, mine, other, head_gains, cos, sin)


def attend_kernel(
    req,
    sources,
    group_ref,
    owner_ref,
    slot_ref,
    q_ref,
    kv_ref,
    wo_ref,
    *refs,
):
    pool_count = len({name for name, _, _, _ in sources})
    pool_refs = refs[:pool_count]
    outs = refs[pool_count:-4]
    keyval, mixed, place, sems = refs[-4:]
    member = lax.axis_index("mlp")
    me = lax.axis_index("req")
    count, head = kv_ref.shape[1], kv_ref.shape[2] // 2
    part = count // 4
    page = pool_refs[0].shape[1]
    n_pages = owner_ref.shape[1]
    per_part = len(sources) // 2
    group = group_ref[req]
    for s in range(len(sources)):
        place[s] = -1
    for i in range(n_pages):
        flip = owner_ref[group, i] ^ me
        far = slot_ref[group, i] ^ (member % 2)
        place[far * per_part + flip] = i
    for name, index, far, flip in sources:
        where = place[far * per_part + flip]

        @pl.when(where >= 0)
        def _():
            start = pl.multiple_of(where * page, page)
            pltpu.make_async_copy(
                pool_refs[name].at[index], keyval.at[pl.ds(start, page), :], sems.at[where]
            ).start()

    pre = n_pages * page
    keyval[pre:, :] = kv_ref[req]
    for i in range(n_pages):
        pltpu.make_async_copy(
            pool_refs[0].at[0], keyval.at[i * page : (i + 1) * page, :], sems.at[i]
        ).wait()

    factor = head**-0.5 * math.log2(math.e)

    def positions(index):
        block = index // part
        flip = (block & 1) * 2 + (block >> 1)
        return (member ^ flip) * part + index % part

    key_at = positions(lax.broadcasted_iota(jnp.int32, (1, count), 1))
    tile = TILE
    heads = q_ref.shape[1] // count
    for first in range(0, count, tile):
        query_at = positions(first + lax.broadcasted_iota(jnp.int32, (tile, 1), 0))
        seen = key_at <= query_at
        for h in range(heads):
            start = h * count + first
            scores = lax.dot_general(
                q_ref[req, start : start + tile, :],
                keyval[:, :head],
                (((1,), (1,)), ((), ())),
                preferred_element_type=F32,
            )
            scores = jnp.concatenate(
                [scores[:, :pre], jnp.where(seen, scores[:, pre:], -jnp.inf)], axis=1
            )
            peak = jnp.max(scores, axis=-1, keepdims=True)
            exps = jnp.exp2((scores - peak) * factor)
            total = jnp.sum(exps, axis=-1, keepdims=True)
            out = jnp.dot(exps.astype(BF16), keyval[:, head:], preferred_element_type=F32)
            mixed[first : first + tile, h * head : (h + 1) * head] = (
                out * (1.0 / total)
            ).astype(BF16)
    width = wo_ref.shape[1]
    step = 512
    for col in range(0, width, step):
        result = jnp.dot(
            mixed[...], wo_ref[:, col : col + step], preferred_element_type=F32
        ).astype(BF16)
        store_rows(outs, col, result)


def store_rows(outs, col, result):
    first = 0
    for out_ref in outs:
        rows = out_ref.shape[0]
        out_ref[:, col : col + result.shape[1]] = result[first : first + rows]
        first += rows


def partial_shapes(part, width):
    return [jax.ShapeDtypeStruct((2 * part, width), BF16)] + [
        jax.ShapeDtypeStruct((part // SPLIT, width), BF16)
    ] * (2 * SPLIT)


def attend(req, sources, group, owner, slot, q, kv, wo, pools):
    count, head = kv.shape[1], kv.shape[2] // 2
    part = count // 4
    heads = q.shape[1] // count
    page = pools[0].shape[1]
    n_pages = owner.shape[1]
    keys = n_pages * page + count
    return pl.pallas_call(
        functools.partial(attend_kernel, req, sources),
        out_shape=partial_shapes(part, wo.shape[1]),
        in_specs=[SCALARS] * 3 + [ON_CHIP] * 3 + [ANYWHERE] * len(pools),
        out_specs=[ON_CHIP] * (1 + 2 * SPLIT),
        scratch_shapes=[
            pltpu.VMEM((keys, 2 * head), BF16),
            pltpu.VMEM((count, heads * head), BF16),
            pltpu.SMEM((len(sources),), jnp.int32),
            pltpu.SemaphoreType.DMA((n_pages,)),
        ],
        compiler_params=params(8),
        cost_estimate=cost(
            heads * count * head * (4 * keys + 2 * wo.shape[1]), 4 << 20, heads * count * keys
        ),
        name="attend",
    )(group, owner, slot, q, kv, wo, *pools)


def pair_kernel(keep_ref, *refs):
    count = 2 * SPLIT
    others, outs = refs[:count], refs[count:]
    total = keep_ref[...].astype(F32) + jnp.concatenate(
        [ref[...].astype(F32) for ref in others], axis=0
    )
    store_rows(outs, 0, total.astype(BF16))


def pair_sum(keep, others, parts):
    rows, width = keep.shape
    return pl.pallas_call(
        pair_kernel,
        out_shape=[jax.ShapeDtypeStruct((rows // parts, width), BF16)] * parts,
        in_specs=[ON_CHIP] * (1 + len(others)),
        out_specs=[ON_CHIP] * parts,
        cost_estimate=cost(2 * keep.size, 6 * keep.size),
        compiler_params=params(6),
        name="pair_sum",
    )(keep, *others)


def residual_kernel(req, own_base_ref, y_base_ref, near_ref, far_ref, gains_ref, res_ref, *in_refs):
    part = res_ref.shape[0]
    for b, base_ref in enumerate((own_base_ref, y_base_ref)):
        mine = slice(b * part, (b + 1) * part)
        theirs = slice((1 - b) * part, (2 - b) * part)
        total = near_ref[mine, :].astype(F32) + far_ref[theirs, :].astype(F32)
        residual = (base_ref[req] + normed(total, gains_ref[2:3, :])) * INV_ROOT
        if b == 0:
            res_ref[...] = residual
        rows = normed(residual, gains_ref[3:4, :]).astype(BF16)
        store_rows(in_refs[b * SPLIT : (b + 1) * SPLIT], 0, rows)


def make_residual(req, own_base, y_base, near, far, gains):
    rows, width = near.shape
    part = rows // 2
    return pl.pallas_call(
        functools.partial(residual_kernel, req),
        out_shape=[
            jax.ShapeDtypeStruct((part, width), F32),
        ]
        + [jax.ShapeDtypeStruct((part // SPLIT, width), BF16)] * (2 * SPLIT),
        in_specs=[ON_CHIP] * 5,
        out_specs=[ON_CHIP] * (1 + 2 * SPLIT),
        cost_estimate=cost(12 * near.size, 16 * near.size),
        compiler_params=params(4),
        name="residual",
    )(own_base, y_base, near, far, gains)


def feed_kernel(gate_ref, up_ref, down_ref, *refs):
    count = 4 * SPLIT
    outs, hidden = refs[count:-1], refs[-1]
    rows = jnp.concatenate([ref[...] for ref in refs[:count]], axis=0)
    units = gate_ref.shape[1]
    step = 512
    for u in range(0, units, step):
        gate = jnp.dot(rows, gate_ref[:, u : u + step], preferred_element_type=F32)
        up = jnp.dot(rows, up_ref[:, u : u + step], preferred_element_type=F32)
        hidden[:, u : u + step] = (jax.nn.gelu(gate, approximate=True) * up).astype(BF16)
    for col in range(0, down_ref.shape[1], step):
        result = jnp.dot(
            hidden[...], down_ref[:, col : col + step], preferred_element_type=F32
        ).astype(BF16)
        store_rows(outs, col, result)


def feed(pieces, gate, up, down):
    width, units = gate.shape
    part = pieces[0].shape[0] * SPLIT
    return pl.pallas_call(
        feed_kernel,
        out_shape=partial_shapes(part, width),
        in_specs=[ON_CHIP] * (3 + len(pieces)),
        out_specs=[ON_CHIP] * (1 + 2 * SPLIT),
        scratch_shapes=[pltpu.VMEM((4 * part, units), BF16)],
        compiler_params=params(8),
        cost_estimate=cost(24 * part * width * units, 12 << 20, 4 * part * units),
        name="feed",
    )(gate, up, down, *pieces)


def finish_kernel(req, len_ref, res_ref, near_ref, far_ref, gains_ref, *refs):
    out_ref = refs[-1]
    part = res_ref.shape[0]
    total = near_ref[...].astype(F32) + far_ref[...].astype(F32)
    output = res_ref[...] + normed(total, gains_ref[4:5, :])
    position = lax.axis_index("mlp") * part + lax.broadcasted_iota(jnp.int32, (part, 1), 0)
    out_ref[0] = jnp.where(position < len_ref[req], output, 0.0).astype(BF16)


def finish(req, reqs, lens, residual, near, far, gains, before):
    part, width = residual.shape
    extra = [] if before is None else [before]
    return pl.pallas_call(
        functools.partial(finish_kernel, req),
        grid=(1,),
        out_shape=jax.ShapeDtypeStruct((reqs, part, width), BF16),
        in_specs=[SCALARS] + [ON_CHIP] * 4 + [ANYWHERE] * len(extra),
        out_specs=pl.BlockSpec((1, part, width), lambda i: (req, 0, 0)),
        input_output_aliases={5: 0} if extra else {},
        cost_estimate=cost(10 * residual.size, 12 * residual.size),
        compiler_params=params(4),
        name="finish",
    )(lens, residual, near, far, gains, *extra)


def local(
    hidden_in,
    input_gain,
    query_weight,
    keyval_weight,
    query_gain,
    key_gain,
    out_weight,
    attn_gain,
    laurel_left,
    laurel_right,
    laurel_gain,
    ffn_gain,
    post_gain,
    gate_projection_matrix,
    up_projection_matrix,
    down_projection_matrix,
    page_pool,
    page_owner,
    page_slot,
    request_group,
    suffix_len,
):
    member = lax.axis_index("mlp")
    part, reqs, width = hidden_in.shape
    head = query_gain.shape[0]
    count = part * lax.axis_size("mlp")
    prefix_len = page_owner.shape[1] * page_pool.shape[1]

    hidden = jnp.transpose(hidden_in, (1, 0, 2))
    gains = jnp.stack([input_gain, laurel_gain, attn_gain, ffn_gain, post_gain])
    head_gains = jnp.stack([query_gain, key_gain])
    half = head // 2
    frequency = 1000000.0 ** (-jnp.arange(half, dtype=F32) / half)
    angles = (prefix_len + jnp.arange(count)).astype(F32)[:, None] * frequency[None, :]
    cos, sin = jnp.cos(angles), jnp.sin(angles)

    page_rows = page_pool.shape[1]
    own_page = lax.dynamic_slice(
        page_pool, (member % 2, 0, member // 2 * 2 * head), (1, page_rows, 2 * head)
    )
    even = list(range(0, lax.axis_size("req"), 2))
    even_pages = [own_page] + [exchange(own_page, "req", flip) for flip in even[1:]]
    hidden_y = exchange(hidden, "mlp", 2)
    hidden_c = exchange(hidden, "mlp", 1)
    other_weight = exchange(after(keyval_weight, hidden_c), "mlp", 1)
    own_base = make_base(hidden, gains, laurel_left.T, laurel_right)
    even_pages[1] = after(even_pages[1], own_base, cos, head_gains)
    even_pages = jnp.concatenate(even_pages)
    odd_pages = exchange(even_pages, "req", 1)
    even_other = exchange(even_pages, "mlp", 1)
    hidden_y = after(hidden_y, even_pages)
    hidden_d = exchange(hidden_y, "mlp", 1)
    y_base = make_base(hidden_y, gains, laurel_left.T, laurel_right)
    pages, q_all, kv_all = project(
        suffix_len,
        hidden,
        after(hidden_y, y_base),
        hidden_c,
        hidden_d,
        gains,
        query_weight,
        keyval_weight,
        other_weight,
        head_gains,
        cos,
        sin,
    )
    odd_pages = after(odd_pages, q_all)
    odd_other = exchange(odd_pages, "mlp", 1)
    pools = [even_pages, odd_pages, even_other, odd_other]
    sources = [
        (p, i, p // 2, flip + p % 2) for p in range(len(pools)) for i, flip in enumerate(even)
    ]

    def attend_one(r, *earlier):
        return attend(
            r,
            sources,
            request_group,
            page_owner,
            page_slot,
            after(q_all, *earlier),
            kv_all,
            out_weight,
            pools,
        )

    def swap(pieces):
        return [exchange(piece, "mlp", 1) for piece in pieces]

    def residual_one(r, *earlier):
        residual, *pieces = make_residual(
            r, own_base, y_base, near[r], after(far[r], *earlier), gains
        )
        residuals[r] = residual
        inputs[r] = pieces + swap(pieces)
        return pieces[0]

    def feed_one(r, *earlier):
        first, *rest = inputs[r]
        return feed(
            [after(first, *earlier), *rest],
            gate_projection_matrix,
            up_projection_matrix,
            down_projection_matrix,
        )

    def finish_one(r, earlier, before):
        near_own, far_own = done[r]
        return finish(
            r,
            reqs,
            suffix_len,
            residuals[r],
            near_own,
            after(far_own, earlier),
            gains,
            before,
        )

    near, far, residuals, inputs = {}, {}, {}, {}
    last = q_all
    for r in range(reqs):
        keep, *pieces = attend_one(r, last)
        others = swap(pieces)
        last = keep
        if r >= 2:
            last = residual_one(r - 2, last)
        (near[r],) = pair_sum(after(keep, last), others, 1)
        far[r] = exchange(near[r], "mlp", 2)
        last = near[r]
    done, result = {}, None
    for r in range(reqs):
        keep, *pieces = feed_one(r, last)
        others = swap(pieces)
        last = keep
        if r + 1 < reqs:
            last = residual_one(r + 1, last)
        else:
            last = result = finish_one(0, last, None)
        near_own, near_y = pair_sum(after(keep, last), others, 2)
        done[r] = (near_own, exchange(near_y, "mlp", 2))
        last = near_own
    for r in range(1, reqs):
        result = finish_one(r, last, result)
    return jnp.transpose(result, (1, 0, 2)), jnp.transpose(pages, (1, 0, 2))


def solution(mesh):
    placed = (
        P("mlp", "req", None),
        P(),
        P(None, "mlp"),
        P(None, "mlp"),
        P(),
        P(),
        P("mlp", None),
        P(),
        P(),
        P(),
        P(),
        P(),
        P(),
        P(None, "mlp"),
        P(None, "mlp"),
        P("mlp", None),
        P("req", None, None),
        P(),
        P(),
        P("req"),
        P("req"),
    )
    return jax.shard_map(
        local,
        mesh=mesh,
        in_specs=placed,
        out_specs=(P("mlp", "req", None), P(None, "req", "mlp")),
        check_vma=False,
    )
```

```python
import functools
import math

import jax
import jax.numpy as jnp
from jax import lax
from jax.experimental import pallas as pl
from jax.experimental.pallas import tpu as pltpu
from jax.sharding import PartitionSpec as P

EPS = 1e-06
INV_ROOT = 1.0 / math.sqrt(2.0)
BF16 = jnp.bfloat16
F32 = jnp.float32
ON_CHIP = pl.BlockSpec(memory_space=pltpu.VMEM)
SCALARS = pl.BlockSpec(memory_space=pltpu.SMEM)
ANYWHERE = pl.BlockSpec(memory_space=pl.ANY)
BLOCK_XOR = (0, 2, 1, 3)
AFTER_ATTEND = (4, 4)
AFTER_FEED = (3, 3, 2)
BEFORE_FEED = (3, 3, 2)
TILE = 256


def exchange(value, axis, flip):
    return lax.ppermute(value, axis, [(i, i ^ flip) for i in range(lax.axis_size(axis))])


def after(value, *earlier):
    return lax.optimization_barrier((value, *earlier))[0]


def normed(values, gain):
    scale = lax.rsqrt(jnp.mean(values * values, axis=-1, keepdims=True) + EPS)
    return values * scale * gain


def rotated(values, cos, sin):
    half = values.shape[-1] // 2
    first, second = values[:, :half], values[:, half:]
    return jnp.concatenate(
        [first * cos - second * sin, second * cos + first * sin], axis=-1
    )


def params(mib):
    return pltpu.CompilerParams(vmem_limit_bytes=mib << 20)


def cost(flops):
    return pl.CostEstimate(flops=int(flops), bytes_accessed=1, transcendentals=0)


def active_rows(hidden, gain):
    return normed(hidden.astype(F32), gain).astype(BF16)


def base_kernel(hidden_ref, gains_ref, left_ref, right_ref, out_ref):
    for r in range(hidden_ref.shape[0]):
        hidden = hidden_ref[r]
        active = active_rows(hidden, gains_ref[0:1, :])
        mid = lax.dot_general(
            active, left_ref[...], (((1,), (1,)), ((), ())), preferred_element_type=F32
        ).astype(BF16)
        low = jnp.dot(mid, right_ref[...], preferred_element_type=F32)
        out_ref[r] = hidden.astype(F32) + active.astype(F32) + normed(low, gains_ref[1:2, :])


def make_base(hidden, gains, left_t, right, flops=1):
    return pl.pallas_call(
        base_kernel,
        out_shape=jax.ShapeDtypeStruct(hidden.shape, F32),
        in_specs=[ON_CHIP] * 4,
        out_specs=ON_CHIP,
        cost_estimate=pl.CostEstimate(flops=int(flops), bytes_accessed=1, transcendentals=0),
        compiler_params=params(8),
        name="base",
    )(hidden, gains, left_t, right)


def project_kernel(
    len_ref,
    hidden_ref,
    y_ref,
    c_ref,
    d_ref,
    gains_ref,
    wq_ref,
    mine_ref,
    other_ref,
    head_gains_ref,
    cos_ref,
    sin_ref,
    page_ref,
    q_ref,
    kv_ref,
):
    member = lax.axis_index("mlp")
    reqs, part, _ = hidden_ref.shape
    head = head_gains_ref.shape[-1]
    qgain, kgain = head_gains_ref[0:1, :], head_gains_ref[1:2, :]
    starts = [pl.multiple_of((member ^ flip) * part, part) for flip in BLOCK_XOR]
    cos = jnp.concatenate([cos_ref[pl.ds(s, part), :] for s in starts], axis=0)
    sin = jnp.concatenate([sin_ref[pl.ds(s, part), :] for s in starts], axis=0)
    holds_keys = member % 2 == 0
    heads = wq_ref.shape[1] // head
    for r in range(reqs):
        rows = jnp.concatenate(
            [
                active_rows(ref[r], gains_ref[0:1, :])
                for ref in (hidden_ref, y_ref, c_ref, d_ref)
            ],
            axis=0,
        )
        count = rows.shape[0]
        mine = jnp.dot(rows, mine_ref[...], preferred_element_type=F32)
        other = jnp.dot(rows, other_ref[...], preferred_element_type=F32)
        keys = rotated(normed(jnp.where(holds_keys, mine, other), kgain), cos, sin)
        values = normed(jnp.where(holds_keys, other, mine), 1.0)
        kv_ref[r, :, :head] = keys.astype(BF16)
        kv_ref[r, :, head:] = values.astype(BF16)
        quarter = jnp.where(holds_keys, keys, values)
        live = len_ref[r]
        for b, start in enumerate(starts):
            position = start + lax.broadcasted_iota(jnp.int32, (part, 1), 0)
            page_ref[r, pl.ds(start, part), :] = jnp.where(
                position < live, quarter[b * part : (b + 1) * part], 0.0
            ).astype(BF16)
        for h in range(heads):
            raw = jnp.dot(
                rows, wq_ref[:, h * head : (h + 1) * head], preferred_element_type=F32
            )
            q_ref[r, h * count : (h + 1) * count, :] = rotated(
                normed(raw, qgain), cos, sin
            ).astype(BF16)


def project(lens, hidden, y, c, d, gains, wq, mine, other, head_gains, cos, sin):
    reqs, part, width = hidden.shape
    count = part * len(BLOCK_XOR)
    head = head_gains.shape[-1]
    heads = wq.shape[1] // head
    return pl.pallas_call(
        project_kernel,
        out_shape=[
            jax.ShapeDtypeStruct((reqs, count, head), BF16),
            jax.ShapeDtypeStruct((reqs, heads * count, head), BF16),
            jax.ShapeDtypeStruct((reqs, count, 2 * head), BF16),
        ],
        in_specs=[SCALARS] + [ON_CHIP] * 11,
        out_specs=[ON_CHIP] * 3,
        compiler_params=params(10),
        cost_estimate=cost(1),
        name="project",
    )(lens, hidden, y, c, d, gains, wq, mine, other, head_gains, cos, sin)


def attend_kernel(
    req,
    sources,
    group_ref,
    owner_ref,
    slot_ref,
    q_ref,
    kv_ref,
    wo_ref,
    *refs,
):
    pool_count = len({name for name, _, _, _ in sources})
    pool_refs = refs[:pool_count]
    outs = refs[pool_count:-4]
    keyval, mixed, place, sems = refs[-4:]
    member = lax.axis_index("mlp")
    me = lax.axis_index("req")
    count, head = kv_ref.shape[1], kv_ref.shape[2] // 2
    part = count // 4
    page = pool_refs[0].shape[1]
    n_pages = owner_ref.shape[1]
    per_part = len(sources) // 2
    group = group_ref[req]
    for s in range(len(sources)):
        place[s] = -1
    for i in range(n_pages):
        flip = owner_ref[group, i] ^ me
        far = slot_ref[group, i] ^ (member % 2)
        place[far * per_part + flip] = i
    for name, index, far, flip in sources:
        where = place[far * per_part + flip]

        @pl.when(where >= 0)
        def _():
            start = pl.multiple_of(where * page, page)
            pltpu.make_async_copy(
                pool_refs[name].at[index], keyval.at[pl.ds(start, page), :], sems.at[where]
            ).start()

    pre = n_pages * page
    keyval[pre:, :] = kv_ref[req]
    for i in range(n_pages):
        pltpu.make_async_copy(
            pool_refs[0].at[0], keyval.at[i * page : (i + 1) * page, :], sems.at[i]
        ).wait()

    factor = head**-0.5 * math.log2(math.e)

    def positions(index):
        block = index // part
        flip = (block & 1) * 2 + (block >> 1)
        return (member ^ flip) * part + index % part

    key_at = positions(lax.broadcasted_iota(jnp.int32, (1, count), 1))
    tile = TILE
    heads = q_ref.shape[1] // count
    for first in range(0, count, tile):
        query_at = positions(first + lax.broadcasted_iota(jnp.int32, (tile, 1), 0))
        seen = key_at <= query_at
        for h in range(heads):
            start = h * count + first
            scores = lax.dot_general(
                q_ref[req, start : start + tile, :],
                keyval[:, :head],
                (((1,), (1,)), ((), ())),
                preferred_element_type=F32,
            )
            scores = jnp.concatenate(
                [scores[:, :pre], jnp.where(seen, scores[:, pre:], -jnp.inf)], axis=1
            )
            peak = jnp.max(scores, axis=-1, keepdims=True)
            exps = jnp.exp2((scores - peak) * factor)
            total = jnp.sum(exps, axis=-1, keepdims=True)
            out = jnp.dot(exps.astype(BF16), keyval[:, head:], preferred_element_type=F32)
            mixed[first : first + tile, h * head : (h + 1) * head] = (
                out * (1.0 / total)
            ).astype(BF16)
    width = wo_ref.shape[1]
    step = 512
    for col in range(0, width, step):
        result = jnp.dot(
            mixed[...], wo_ref[:, col : col + step], preferred_element_type=F32
        ).astype(BF16)
        store_rows(outs, col, result)


def store_rows(outs, col, result):
    first = 0
    for out_ref in outs:
        rows = out_ref.shape[0]
        out_ref[:, col : col + result.shape[1]] = result[first : first + rows]
        first += rows


def piece_shapes(part, width, pieces):
    return [jax.ShapeDtypeStruct((part // 4 * piece, width), BF16) for piece in pieces]


def partial_shapes(part, width, pieces):
    kept = jax.ShapeDtypeStruct((2 * part, width), BF16)
    return [kept] + piece_shapes(part, width, pieces)


def attend(req, sources, group, owner, slot, q, kv, wo, pools):
    count, head = kv.shape[1], kv.shape[2] // 2
    part = count // 4
    heads = q.shape[1] // count
    page = pools[0].shape[1]
    n_pages = owner.shape[1]
    keys = n_pages * page + count
    return pl.pallas_call(
        functools.partial(attend_kernel, req, sources),
        out_shape=partial_shapes(part, wo.shape[1], AFTER_ATTEND),
        in_specs=[SCALARS] * 3 + [ON_CHIP] * 3 + [ANYWHERE] * len(pools),
        out_specs=[ON_CHIP] * (1 + len(AFTER_ATTEND)),
        scratch_shapes=[
            pltpu.VMEM((keys, 2 * head), BF16),
            pltpu.VMEM((count, heads * head), BF16),
            pltpu.SMEM((len(sources),), jnp.int32),
            pltpu.SemaphoreType.DMA((n_pages,)),
        ],
        compiler_params=params(8),
        cost_estimate=cost(1),
        name="attend",
    )(group, owner, slot, q, kv, wo, *pools)


def pair_kernel(count, keep_ref, *refs):
    others, outs = refs[:count], refs[count:]
    total = keep_ref[...].astype(F32) + jnp.concatenate(
        [ref[...].astype(F32) for ref in others], axis=0
    )
    store_rows(outs, 0, total.astype(BF16))


def pair_sum(keep, others, parts):
    rows, width = keep.shape
    return pl.pallas_call(
        functools.partial(pair_kernel, len(others)),
        out_shape=[jax.ShapeDtypeStruct((rows // parts, width), BF16)] * parts,
        in_specs=[ON_CHIP] * (1 + len(others)),
        out_specs=[ON_CHIP] * parts,
        cost_estimate=cost(1),
        compiler_params=params(6),
        name="pair_sum",
    )(keep, *others)


def residual_kernel(req, own_base_ref, y_base_ref, near_ref, far_ref, gains_ref, res_ref, *in_refs):
    part = res_ref.shape[0]
    blocks = []
    for b, base_ref in enumerate((own_base_ref, y_base_ref)):
        mine = slice(b * part, (b + 1) * part)
        theirs = slice((1 - b) * part, (2 - b) * part)
        total = near_ref[mine, :].astype(F32) + far_ref[theirs, :].astype(F32)
        residual = (base_ref[req] + normed(total, gains_ref[2:3, :])) * INV_ROOT
        if b == 0:
            res_ref[...] = residual
        blocks.append(normed(residual, gains_ref[3:4, :]).astype(BF16))
    store_rows(in_refs, 0, jnp.concatenate(blocks, axis=0))


def make_residual(req, own_base, y_base, near, far, gains):
    rows, width = near.shape
    part = rows // 2
    return pl.pallas_call(
        functools.partial(residual_kernel, req),
        out_shape=[
            jax.ShapeDtypeStruct((part, width), F32),
        ]
        + piece_shapes(part, width, BEFORE_FEED),
        in_specs=[ON_CHIP] * 5,
        out_specs=[ON_CHIP] * (1 + len(BEFORE_FEED)),
        cost_estimate=cost(1e11),
        compiler_params=params(4),
        name="residual",
    )(own_base, y_base, near, far, gains)


def feed_kernel(count, gate_ref, up_ref, down_ref, *refs):
    outs, hidden = refs[count:-1], refs[-1]
    rows = jnp.concatenate([ref[...] for ref in refs[:count]], axis=0)
    units = gate_ref.shape[1]
    step = 512
    for u in range(0, units, step):
        gate = jnp.dot(rows, gate_ref[:, u : u + step], preferred_element_type=F32)
        up = jnp.dot(rows, up_ref[:, u : u + step], preferred_element_type=F32)
        hidden[:, u : u + step] = (jax.nn.gelu(gate, approximate=True) * up).astype(BF16)
    for col in range(0, down_ref.shape[1], step):
        result = jnp.dot(
            hidden[...], down_ref[:, col : col + step], preferred_element_type=F32
        ).astype(BF16)
        store_rows(outs, col, result)


def feed(pieces, gate, up, down):
    width, units = gate.shape
    part = sum(piece.shape[0] for piece in pieces) // 4
    return pl.pallas_call(
        functools.partial(feed_kernel, len(pieces)),
        out_shape=partial_shapes(part, width, AFTER_FEED),
        in_specs=[ON_CHIP] * (3 + len(pieces)),
        out_specs=[ON_CHIP] * (1 + len(AFTER_FEED)),
        scratch_shapes=[pltpu.VMEM((4 * part, units), BF16)],
        compiler_params=params(8),
        cost_estimate=cost(1),
        name="feed",
    )(gate, up, down, *pieces)


def finish_kernel(req, len_ref, res_ref, near_ref, far_ref, gains_ref, *refs):
    out_ref = refs[-1]
    part = res_ref.shape[0]
    total = near_ref[...].astype(F32) + far_ref[...].astype(F32)
    output = res_ref[...] + normed(total, gains_ref[4:5, :])
    position = lax.axis_index("mlp") * part + lax.broadcasted_iota(jnp.int32, (part, 1), 0)
    out_ref[0] = jnp.where(position < len_ref[req], output, 0.0).astype(BF16)


def finish(req, reqs, lens, residual, near, far, gains, before):
    part, width = residual.shape
    extra = [] if before is None else [before]
    return pl.pallas_call(
        functools.partial(finish_kernel, req),
        grid=(1,),
        out_shape=jax.ShapeDtypeStruct((reqs, part, width), BF16),
        in_specs=[SCALARS] + [ON_CHIP] * 4 + [ANYWHERE] * len(extra),
        out_specs=pl.BlockSpec((1, part, width), lambda i: (req, 0, 0)),
        input_output_aliases={5: 0} if extra else {},
        cost_estimate=cost(1e11),
        compiler_params=params(4),
        name="finish",
    )(lens, residual, near, far, gains, *extra)


def local(
    hidden_in,
    input_gain,
    query_weight,
    keyval_weight,
    query_gain,
    key_gain,
    out_weight,
    attn_gain,
    laurel_left,
    laurel_right,
    laurel_gain,
    ffn_gain,
    post_gain,
    gate_projection_matrix,
    up_projection_matrix,
    down_projection_matrix,
    page_pool,
    page_owner,
    page_slot,
    request_group,
    suffix_len,
):
    member = lax.axis_index("mlp")
    part, reqs, width = hidden_in.shape
    head = query_gain.shape[0]
    count = part * lax.axis_size("mlp")
    prefix_len = page_owner.shape[1] * page_pool.shape[1]

    hidden = jnp.transpose(hidden_in, (1, 0, 2))
    gains = jnp.stack([input_gain, laurel_gain, attn_gain, ffn_gain, post_gain])
    head_gains = jnp.stack([query_gain, key_gain])
    half = head // 2
    frequency = 1000000.0 ** (-jnp.arange(half, dtype=F32) / half)
    angles = (prefix_len + jnp.arange(count)).astype(F32)[:, None] * frequency[None, :]
    cos, sin = jnp.cos(angles), jnp.sin(angles)

    hidden_y = exchange(hidden, "mlp", 2)
    hidden_c = exchange(hidden, "mlp", 1)

    page_rows = page_pool.shape[1]
    own_page = lax.dynamic_slice(
        after(page_pool, hidden_c), (member % 2, 0, member // 2 * 2 * head), (1, page_rows, 2 * head)
    )
    later = list(range(4, lax.axis_size("req"), 2))
    direct = {flip: exchange(own_page, "req", flip) for flip in [*later, 2]}
    other_weight = exchange(after(keyval_weight, hidden_c), "mlp", 1)
    near_pages = jnp.concatenate([own_page, after(direct[2], cos, gains, head_gains)])
    near_odd = exchange(near_pages, "req", 1)
    own_base = make_base(after(hidden, near_pages), gains, laurel_left.T, laurel_right)
    far_pages = [direct[flip] for flip in later]
    far_pages[0] = after(far_pages[0], own_base)
    far_pages = jnp.concatenate(far_pages)
    far_odd = exchange(far_pages, "req", 1)
    far_other = exchange(far_pages, "mlp", 1)
    near_other = exchange(near_pages, "mlp", 1)
    hidden_y = after(hidden_y, far_pages)
    hidden_d = exchange(hidden_y, "mlp", 1)
    y_base = make_base(hidden_y, gains, laurel_left.T, laurel_right, 1e11)
    pages, q_all, kv_all = project(
        suffix_len,
        hidden,
        after(hidden_y, y_base),
        hidden_c,
        hidden_d,
        gains,
        query_weight,
        keyval_weight,
        other_weight,
        head_gains,
        cos,
        sin,
    )
    near_odd = after(near_odd, q_all)
    near_odd_other = exchange(near_odd, "mlp", 1)
    far_odd = after(far_odd, q_all)
    far_odd_other = exchange(far_odd, "mlp", 1)
    pools = [near_pages, far_pages, near_odd, far_odd]
    pools += [near_other, far_other, near_odd_other, far_odd_other]
    flips = [[0, 2], later, [1, 3], [flip + 1 for flip in later]]
    sources = [
        (p, i, p // 4, flip) for p in range(len(pools)) for i, flip in enumerate(flips[p % 4])
    ]

    def attend_one(r, *earlier):
        return attend(
            r,
            sources,
            request_group,
            page_owner,
            page_slot,
            after(q_all, *earlier),
            kv_all,
            out_weight,
            pools,
        )

    def swap(pieces):
        return [exchange(piece, "mlp", 1) for piece in pieces]

    def residual_one(r, *earlier):
        residual, *pieces = make_residual(
            r, own_base, y_base, near[r], after(far[r], *earlier), gains
        )
        residuals[r] = residual
        inputs[r] = pieces + swap(pieces)
        return pieces[0]

    def feed_one(r, *earlier):
        first, *rest = inputs[r]
        return feed(
            [after(first, *earlier), *rest],
            gate_projection_matrix,
            up_projection_matrix,
            down_projection_matrix,
        )

    def finish_one(r, earlier, before):
        near_own, far_own = done[r]
        return finish(
            r,
            reqs,
            suffix_len,
            residuals[r],
            near_own,
            after(far_own, earlier),
            gains,
            before,
        )

    near, far, residuals, inputs = {}, {}, {}, {}
    last = q_all
    for r in range(reqs):
        keep, *pieces = attend_one(r, last)
        others = swap(pieces)
        last = keep
        if r >= 2:
            last = residual_one(r - 2, last)
        (near[r],) = pair_sum(after(keep, last), others, 1)
        far[r] = exchange(near[r], "mlp", 2)
        last = near[r]
    done, result = {}, None
    for r in range(reqs):
        keep, *pieces = feed_one(r, last)
        others = swap(pieces)
        last = keep
        if r + 1 < reqs:
            last = residual_one(r + 1, last)
        else:
            last = result = finish_one(0, last, None)
        near_own, near_y = pair_sum(after(keep, last), others, 2)
        done[r] = (near_own, exchange(near_y, "mlp", 2))
        last = near_own
    for r in range(1, reqs):
        result = finish_one(r, last, result)
    return jnp.transpose(result, (1, 0, 2)), jnp.transpose(pages, (1, 0, 2))


def solution(mesh):
    placed = (
        P("mlp", "req", None),
        P(),
        P(None, "mlp"),
        P(None, "mlp"),
        P(),
        P(),
        P("mlp", None),
        P(),
        P(),
        P(),
        P(),
        P(),
        P(),
        P(None, "mlp"),
        P(None, "mlp"),
        P("mlp", None),
        P("req", None, None),
        P(),
        P(),
        P("req"),
        P("req"),
    )
    return jax.shard_map(
        local,
        mesh=mesh,
        in_specs=placed,
        out_specs=(P("mlp", "req", None), P(None, "req", "mlp")),
        check_vma=False,
    )
```

```python
import functools
import math

import jax
import jax.numpy as jnp
from jax import lax
from jax.experimental import pallas as pl
from jax.experimental.pallas import tpu as pltpu
from jax.sharding import PartitionSpec as P

EPS = 1e-06
INV_ROOT = 1.0 / math.sqrt(2.0)
BF16 = jnp.bfloat16
F32 = jnp.float32
ON_CHIP = pl.BlockSpec(memory_space=pltpu.VMEM)
SCALARS = pl.BlockSpec(memory_space=pltpu.SMEM)
ANYWHERE = pl.BlockSpec(memory_space=pl.ANY)
BLOCK_XOR = (0, 2, 1, 3)
AFTER_ATTEND = (4, 4)
AFTER_FEED = (3, 3, 2)
BEFORE_FEED = (3, 3, 2)
TILE = 256
FIRST_CUT = 1


def exchange(value, axis, flip):
    return lax.ppermute(value, axis, [(i, i ^ flip) for i in range(lax.axis_size(axis))])


def after(value, *earlier):
    return lax.optimization_barrier((value, *earlier))[0]


def normed(values, gain):
    scale = lax.rsqrt(jnp.mean(values * values, axis=-1, keepdims=True) + EPS)
    return values * scale * gain


def rotated(values, cos, sin):
    half = values.shape[-1] // 2
    first, second = values[:, :half], values[:, half:]
    return jnp.concatenate(
        [first * cos - second * sin, second * cos + first * sin], axis=-1
    )


def params(mib):
    return pltpu.CompilerParams(vmem_limit_bytes=mib << 20)


def cost(flops):
    return pl.CostEstimate(flops=int(flops), bytes_accessed=1, transcendentals=0)


def active_rows(hidden, gain):
    return normed(hidden.astype(F32), gain).astype(BF16)


def base_kernel(hidden_ref, gains_ref, left_ref, right_ref, out_ref):
    for r in range(hidden_ref.shape[0]):
        hidden = hidden_ref[r]
        active = active_rows(hidden, gains_ref[0:1, :])
        mid = lax.dot_general(
            active, left_ref[...], (((1,), (1,)), ((), ())), preferred_element_type=F32
        ).astype(BF16)
        low = jnp.dot(mid, right_ref[...], preferred_element_type=F32)
        out_ref[r] = hidden.astype(F32) + active.astype(F32) + normed(low, gains_ref[1:2, :])


def make_base(hidden, gains, left_t, right, flops=1):
    return pl.pallas_call(
        base_kernel,
        out_shape=jax.ShapeDtypeStruct(hidden.shape, F32),
        in_specs=[ON_CHIP] * 4,
        out_specs=ON_CHIP,
        cost_estimate=pl.CostEstimate(flops=int(flops), bytes_accessed=1, transcendentals=0),
        compiler_params=params(8),
        name="base",
    )(hidden, gains, left_t, right)


def project_kernel(
    reqs,
    pages_in,
    len_ref,
    hidden_ref,
    y_ref,
    c_ref,
    d_ref,
    gains_ref,
    wq_ref,
    wkv_ref,
    head_gains_ref,
    cos_ref,
    sin_ref,
    *refs,
):
    page_ref, q_ref, quarter_ref = refs[pages_in:]
    member = lax.axis_index("mlp")
    part = hidden_ref.shape[1]
    head = head_gains_ref.shape[-1]
    qgain, kgain = head_gains_ref[0:1, :], head_gains_ref[1:2, :]
    starts = [pl.multiple_of((member ^ flip) * part, part) for flip in BLOCK_XOR]
    cos = jnp.concatenate([cos_ref[pl.ds(s, part), :] for s in starts], axis=0)
    sin = jnp.concatenate([sin_ref[pl.ds(s, part), :] for s in starts], axis=0)
    holds_keys = member % 2 == 0
    heads = wq_ref.shape[1] // head
    for i, r in enumerate(reqs):
        rows = jnp.concatenate(
            [
                active_rows(ref[r], gains_ref[0:1, :])
                for ref in (hidden_ref, y_ref, c_ref, d_ref)
            ],
            axis=0,
        )
        count = rows.shape[0]
        raw = jnp.dot(rows, wkv_ref[...], preferred_element_type=F32)
        quarter = jnp.where(holds_keys, rotated(normed(raw, kgain), cos, sin), normed(raw, 1.0))
        quarter_ref[i] = quarter.astype(BF16)
        live = len_ref[r]
        for b, start in enumerate(starts):
            position = start + lax.broadcasted_iota(jnp.int32, (part, 1), 0)
            page_ref[i, pl.ds(start, part), :] = jnp.where(
                position < live, quarter[b * part : (b + 1) * part], 0.0
            ).astype(BF16)
        for h in range(heads):
            raw = jnp.dot(
                rows, wq_ref[:, h * head : (h + 1) * head], preferred_element_type=F32
            )
            q_ref[i, h * count : (h + 1) * count, :] = rotated(
                normed(raw, qgain), cos, sin
            ).astype(BF16)


def project(reqs, pages, lens, hidden, y, c, d, gains, wq, wkv, head_gains, cos, sin):
    part = hidden.shape[1]
    count = part * len(BLOCK_XOR)
    head = head_gains.shape[-1]
    heads = wq.shape[1] // head
    here = len(reqs)
    extra = [] if pages is None else [pages]
    return pl.pallas_call(
        functools.partial(project_kernel, reqs, len(extra)),
        grid=(1,),
        out_shape=[
            jax.ShapeDtypeStruct((hidden.shape[0], count, head), BF16),
            jax.ShapeDtypeStruct((here, heads * count, head), BF16),
            jax.ShapeDtypeStruct((here, count, head), BF16),
        ],
        in_specs=[SCALARS] + [ON_CHIP] * 10 + [ANYWHERE] * len(extra),
        out_specs=[
            pl.BlockSpec((here, count, head), lambda i: (reqs[0] // here, 0, 0)),
            ON_CHIP,
            ON_CHIP,
        ],
        input_output_aliases={11: 0} if extra else {},
        compiler_params=params(10),
        cost_estimate=cost(1),
        name="project",
    )(lens, hidden, y, c, d, gains, wq, wkv, head_gains, cos, sin, *extra)


def attend_kernel(
    req,
    index,
    offset,
    rows,
    sources,
    group_ref,
    owner_ref,
    slot_ref,
    q_ref,
    mine_ref,
    other_ref,
    wo_ref,
    *refs,
):
    pool_count = len({name for name, _, _, _ in sources})
    pool_refs = refs[:pool_count]
    outs = refs[pool_count:-4]
    keyval, mixed, place, sems = refs[-4:]
    member = lax.axis_index("mlp")
    me = lax.axis_index("req")
    count, head = mine_ref.shape[1:]
    part = count // len(BLOCK_XOR)
    page = pool_refs[0].shape[1]
    n_pages = owner_ref.shape[1]
    per_part = len(sources) // 2
    group = group_ref[req]
    for s in range(len(sources)):
        place[s] = -1
    for i in range(n_pages):
        flip = owner_ref[group, i] ^ me
        far = slot_ref[group, i] ^ (member % 2)
        place[far * per_part + flip] = i
    for name, entry, far, flip in sources:
        where = place[far * per_part + flip]

        @pl.when(where >= 0)
        def _():
            start = pl.multiple_of(where * page, page)
            pltpu.make_async_copy(
                pool_refs[name].at[entry], keyval.at[pl.ds(start, page), :], sems.at[where]
            ).start()

    pre = n_pages * page
    holds_keys = member % 2 == 0

    half = count // 2

    def place_suffix(mine_cols, other_cols):
        keyval[pre:, mine_cols] = mine_ref[index]
        keyval[pre : pre + half, other_cols] = other_ref[index, half:, :]
        keyval[pre + half :, other_cols] = other_ref[index, :half, :]

    @pl.when(holds_keys)
    def _():
        place_suffix(slice(0, head), slice(head, 2 * head))

    @pl.when(jnp.logical_not(holds_keys))
    def _():
        place_suffix(slice(head, 2 * head), slice(0, head))

    for i in range(n_pages):
        pltpu.make_async_copy(
            pool_refs[0].at[0], keyval.at[i * page : (i + 1) * page, :], sems.at[i]
        ).wait()

    factor = head**-0.5 * math.log2(math.e)
    column = lax.broadcasted_iota(jnp.int32, (1, count), 1)
    block = column // part
    key_at = (member ^ ((block & 1) * 2 + (block >> 1))) * part + column % part
    heads = q_ref.shape[1] // count
    pieces = [(h, b) for h in range(heads) for b in range(len(BLOCK_XOR))]
    per_step = max(1, TILE // rows)
    for first in range(0, len(pieces), per_step):
        step = pieces[first : first + per_step]
        starts = [h * count + b * part + offset for h, b in step]
        queries = jnp.concatenate([q_ref[index, s : s + rows, :] for s in starts], axis=0)
        query_at = jnp.concatenate(
            [
                (member ^ BLOCK_XOR[b]) * part
                + offset
                + lax.broadcasted_iota(jnp.int32, (rows, 1), 0)
                for _, b in step
            ],
            axis=0,
        )
        scores = lax.dot_general(
            queries,
            keyval[:, :head],
            (((1,), (1,)), ((), ())),
            preferred_element_type=F32,
        )
        scores = jnp.concatenate(
            [scores[:, :pre], jnp.where(key_at <= query_at, scores[:, pre:], -jnp.inf)], axis=1
        )
        peak = jnp.max(scores, axis=-1, keepdims=True)
        exps = jnp.exp2((scores - peak) * factor)
        total = jnp.sum(exps, axis=-1, keepdims=True)
        out = jnp.dot(exps.astype(BF16), keyval[:, head:], preferred_element_type=F32)
        out = (out * (1.0 / total)).astype(BF16)
        for i, (h, b) in enumerate(step):
            mixed[b * rows : (b + 1) * rows, h * head : (h + 1) * head] = out[
                i * rows : (i + 1) * rows
            ]
    width = wo_ref.shape[1]
    step = 512
    for col in range(0, width, step):
        result = jnp.dot(
            mixed[...], wo_ref[:, col : col + step], preferred_element_type=F32
        ).astype(BF16)
        store_rows(outs, col, result)


def store_rows(outs, col, result):
    first = 0
    for out_ref in outs:
        rows = out_ref.shape[0]
        out_ref[:, col : col + result.shape[1]] = result[first : first + rows]
        first += rows


def piece_shapes(part, width, pieces):
    return [jax.ShapeDtypeStruct((part // 4 * piece, width), BF16) for piece in pieces]


def partial_shapes(part, width, pieces):
    kept = jax.ShapeDtypeStruct((2 * part, width), BF16)
    return [kept] + piece_shapes(part, width, pieces)


def attend(req, index, offset, rows, sources, group, owner, slot, q, mine, other, wo, pools):
    count, head = mine.shape[1:]
    heads = q.shape[1] // count
    page = pools[0].shape[1]
    n_pages = owner.shape[1]
    keys = n_pages * page + count
    return pl.pallas_call(
        functools.partial(attend_kernel, req, index, offset, rows, sources),
        out_shape=partial_shapes(rows, wo.shape[1], AFTER_ATTEND),
        in_specs=[SCALARS] * 3 + [ON_CHIP] * 4 + [ANYWHERE] * len(pools),
        out_specs=[ON_CHIP] * (1 + len(AFTER_ATTEND)),
        scratch_shapes=[
            pltpu.VMEM((keys, 2 * head), BF16),
            pltpu.VMEM((len(BLOCK_XOR) * rows, heads * head), BF16),
            pltpu.SMEM((len(sources),), jnp.int32),
            pltpu.SemaphoreType.DMA((n_pages,)),
        ],
        compiler_params=params(8),
        cost_estimate=cost(1),
        name="attend",
    )(group, owner, slot, q, mine, other, wo, *pools)


def pair_kernel(count, keep_ref, *refs):
    others, outs = refs[:count], refs[count:]
    total = keep_ref[...].astype(F32) + jnp.concatenate(
        [ref[...].astype(F32) for ref in others], axis=0
    )
    store_rows(outs, 0, total.astype(BF16))


def pair_sum(keep, others, parts):
    rows, width = keep.shape
    return pl.pallas_call(
        functools.partial(pair_kernel, len(others)),
        out_shape=[jax.ShapeDtypeStruct((rows // parts, width), BF16)] * parts,
        in_specs=[ON_CHIP] * (1 + len(others)),
        out_specs=[ON_CHIP] * parts,
        cost_estimate=cost(1),
        compiler_params=params(6),
        name="pair_sum",
    )(keep, *others)


def residual_kernel(req, count, gains_ref, own_base_ref, y_base_ref, *refs):
    near_refs, far_refs = refs[:count], refs[count : 2 * count]
    res_ref, in_refs = refs[2 * count], refs[2 * count + 1 :]
    blocks = []
    for b, base_ref in enumerate((own_base_ref, y_base_ref)):
        sums = []
        for near_ref, far_ref in zip(near_refs, far_refs):
            rows = near_ref.shape[0] // 2
            mine = slice(b * rows, (b + 1) * rows)
            theirs = slice((1 - b) * rows, (2 - b) * rows)
            sums.append(near_ref[mine, :].astype(F32) + far_ref[theirs, :].astype(F32))
        total = jnp.concatenate(sums, axis=0)
        residual = (base_ref[req] + normed(total, gains_ref[2:3, :])) * INV_ROOT
        if b == 0:
            res_ref[...] = residual
        blocks.append(normed(residual, gains_ref[3:4, :]).astype(BF16))
    store_rows(in_refs, 0, jnp.concatenate(blocks, axis=0))


def make_residual(req, gains, own_base, y_base, near, far):
    part, width = own_base.shape[1:]
    return pl.pallas_call(
        functools.partial(residual_kernel, req, len(near)),
        out_shape=[jax.ShapeDtypeStruct((part, width), F32)]
        + piece_shapes(part, width, BEFORE_FEED),
        in_specs=[ON_CHIP] * (3 + 2 * len(near)),
        out_specs=[ON_CHIP] * (1 + len(BEFORE_FEED)),
        cost_estimate=cost(1e11),
        compiler_params=params(4),
        name="residual",
    )(gains, own_base, y_base, *near, *far)


def feed_kernel(count, gate_ref, up_ref, down_ref, *refs):
    outs, hidden = refs[count:-1], refs[-1]
    rows = jnp.concatenate([ref[...] for ref in refs[:count]], axis=0)
    units = gate_ref.shape[1]
    step = 512
    for u in range(0, units, step):
        gate = jnp.dot(rows, gate_ref[:, u : u + step], preferred_element_type=F32)
        up = jnp.dot(rows, up_ref[:, u : u + step], preferred_element_type=F32)
        hidden[:, u : u + step] = (jax.nn.gelu(gate, approximate=True) * up).astype(BF16)
    for col in range(0, down_ref.shape[1], step):
        result = jnp.dot(
            hidden[...], down_ref[:, col : col + step], preferred_element_type=F32
        ).astype(BF16)
        store_rows(outs, col, result)


def feed(pieces, gate, up, down):
    width, units = gate.shape
    part = sum(piece.shape[0] for piece in pieces) // 4
    return pl.pallas_call(
        functools.partial(feed_kernel, len(pieces)),
        out_shape=partial_shapes(part, width, AFTER_FEED),
        in_specs=[ON_CHIP] * (3 + len(pieces)),
        out_specs=[ON_CHIP] * (1 + len(AFTER_FEED)),
        scratch_shapes=[pltpu.VMEM((4 * part, units), BF16)],
        compiler_params=params(8),
        cost_estimate=cost(1),
        name="feed",
    )(gate, up, down, *pieces)


def finish_kernel(req, len_ref, res_ref, near_ref, far_ref, gains_ref, *refs):
    out_ref = refs[-1]
    part = res_ref.shape[0]
    total = near_ref[...].astype(F32) + far_ref[...].astype(F32)
    output = res_ref[...] + normed(total, gains_ref[4:5, :])
    position = lax.axis_index("mlp") * part + lax.broadcasted_iota(jnp.int32, (part, 1), 0)
    out_ref[0] = jnp.where(position < len_ref[req], output, 0.0).astype(BF16)


def finish(req, reqs, lens, residual, near, far, gains, before):
    part, width = residual.shape
    extra = [] if before is None else [before]
    return pl.pallas_call(
        functools.partial(finish_kernel, req),
        grid=(1,),
        out_shape=jax.ShapeDtypeStruct((reqs, part, width), BF16),
        in_specs=[SCALARS] + [ON_CHIP] * 4 + [ANYWHERE] * len(extra),
        out_specs=pl.BlockSpec((1, part, width), lambda i: (req, 0, 0)),
        input_output_aliases={5: 0} if extra else {},
        cost_estimate=cost(1e11 if req == 0 else 1),
        compiler_params=params(4),
        name="finish",
    )(lens, residual, near, far, gains, *extra)


def local(
    hidden_in,
    input_gain,
    query_weight,
    keyval_weight,
    query_gain,
    key_gain,
    out_weight,
    attn_gain,
    laurel_left,
    laurel_right,
    laurel_gain,
    ffn_gain,
    post_gain,
    gate_projection_matrix,
    up_projection_matrix,
    down_projection_matrix,
    page_pool,
    page_owner,
    page_slot,
    request_group,
    suffix_len,
):
    member = lax.axis_index("mlp")
    part, reqs, width = hidden_in.shape
    head = query_gain.shape[0]
    count = part * lax.axis_size("mlp")
    prefix_len = page_owner.shape[1] * page_pool.shape[1]

    hidden = jnp.transpose(hidden_in, (1, 0, 2))
    gains = jnp.stack([input_gain, laurel_gain, attn_gain, ffn_gain, post_gain])
    head_gains = jnp.stack([query_gain, key_gain])
    half = head // 2
    frequency = 1000000.0 ** (-jnp.arange(half, dtype=F32) / half)
    angles = (prefix_len + jnp.arange(count)).astype(F32)[:, None] * frequency[None, :]
    cos, sin = jnp.cos(angles), jnp.sin(angles)

    hidden_y = exchange(hidden, "mlp", 2)
    hidden_c = exchange(hidden, "mlp", 1)

    page_rows = page_pool.shape[1]
    own_page = lax.dynamic_slice(
        after(page_pool, hidden_c), (member % 2, 0, member // 2 * 2 * head), (1, page_rows, 2 * head)
    )
    later = list(range(4, lax.axis_size("req"), 2))
    direct = {flip: exchange(own_page, "req", flip) for flip in [*later, 2]}
    near_pages = jnp.concatenate([own_page, after(direct[2], cos, gains, head_gains)])
    near_odd = exchange(near_pages, "req", 1)
    own_base = make_base(after(hidden, near_pages), gains, laurel_left.T, laurel_right)
    far_pages = [direct[flip] for flip in later]
    far_pages[0] = after(far_pages[0], own_base)
    far_pages = jnp.concatenate(far_pages)
    far_odd = exchange(far_pages, "req", 1)
    far_other = exchange(far_pages, "mlp", 1)
    near_other = exchange(near_pages, "mlp", 1)
    hidden_y = after(hidden_y, far_pages)
    hidden_d = exchange(hidden_y, "mlp", 1)
    y_base = make_base(hidden_y, gains, laurel_left.T, laurel_right, 1e11)
    hidden_y = after(hidden_y, y_base)

    def project_some(some, pages, *earlier):
        return project(
            some,
            pages,
            suffix_len,
            after(hidden, *earlier),
            hidden_y,
            hidden_c,
            hidden_d,
            gains,
            query_weight,
            keyval_weight,
            head_gains,
            cos,
            sin,
        )

    pages, q_first, kv_first = project_some([0], None)
    projected = [(q_first, kv_first, exchange(kv_first, "mlp", 1), 0)]
    near_odd = after(near_odd, q_first)
    near_odd_other = exchange(near_odd, "mlp", 1)
    far_odd = after(far_odd, q_first)
    far_odd_other = exchange(far_odd, "mlp", 1)
    pools = [near_pages, far_pages, near_odd, far_odd]
    pools += [near_other, far_other, near_odd_other, far_odd_other]
    flips = [[0, 2], later, [1, 3], [flip + 1 for flip in later]]
    sources = [
        (p, i, p // 4, flip) for p in range(len(pools)) for i, flip in enumerate(flips[p % 4])
    ]

    pages, q_next, kv_next = project_some([1], pages, q_first)
    projected.append((q_next, kv_next, exchange(kv_next, "mlp", 1), 0))

    def attend_one(r, offset, rows, *earlier):
        q, mine, other, index = projected[r]
        return attend(
            r,
            index,
            offset,
            rows,
            sources,
            request_group,
            page_owner,
            page_slot,
            after(q, *earlier),
            mine,
            other,
            out_weight,
            pools,
        )

    def swap(pieces):
        return [exchange(piece, "mlp", 1) for piece in pieces]

    def residual_one(r, *earlier):
        first, *rest = far[r]
        residual, *pieces = make_residual(
            r, gains, own_base, y_base, near[r], [after(first, *earlier), *rest]
        )
        residuals[r] = residual
        inputs[r] = pieces + swap(pieces)
        return pieces[0]

    def feed_one(r, *earlier):
        first, *rest = inputs[r]
        return feed(
            [after(first, *earlier), *rest],
            gate_projection_matrix,
            up_projection_matrix,
            down_projection_matrix,
        )

    def finish_one(r, earlier, before):
        near_own, far_own = done[r]
        return finish(
            r,
            reqs,
            suffix_len,
            residuals[r],
            near_own,
            after(far_own, earlier),
            gains,
            before,
        )

    near, far, residuals, inputs = {}, {}, {}, {}
    last = q_next
    for r in range(reqs):
        rows = part // FIRST_CUT if r == 0 else part
        near[r], far[r] = [], []
        for offset in range(0, part, rows):
            keep, *pieces = attend_one(r, offset, rows, last)
            others = swap(pieces)
            last = keep
            if r >= 2:
                last = residual_one(r - 2, last)
            (joined,) = pair_sum(after(keep, last), others, 1)
            near[r].append(joined)
            far[r].append(exchange(joined, "mlp", 2))
            last = joined
        if r + 2 < reqs:
            pages, q_next, kv_next = project_some([r + 2], pages, last)
            projected.append((q_next, kv_next, exchange(kv_next, "mlp", 1), 0))
            last = q_next
    done, result = {}, None
    for r in range(reqs):
        keep, *pieces = feed_one(r, last)
        others = swap(pieces)
        last = keep
        if r + 1 < reqs:
            last = residual_one(r + 1, last)
        else:
            last = result = finish_one(0, last, None)
        near_own, near_y = pair_sum(after(keep, last), others, 2)
        done[r] = (near_own, exchange(near_y, "mlp", 2))
        last = near_own
    for r in range(1, reqs):
        result = finish_one(r, last, result)
    return jnp.transpose(result, (1, 0, 2)), jnp.transpose(pages, (1, 0, 2))


def solution(mesh):
    placed = (
        P("mlp", "req", None),
        P(),
        P(None, "mlp"),
        P(None, "mlp"),
        P(),
        P(),
        P("mlp", None),
        P(),
        P(),
        P(),
        P(),
        P(),
        P(),
        P(None, "mlp"),
        P(None, "mlp"),
        P("mlp", None),
        P("req", None, None),
        P(),
        P(),
        P("req"),
        P("req"),
    )
    return jax.shard_map(
        local,
        mesh=mesh,
        in_specs=placed,
        out_specs=(P("mlp", "req", None), P(None, "req", "mlp")),
        check_vma=False,
    )
```

```python
import functools
import math

import jax
import jax.numpy as jnp
from jax import lax
from jax.experimental import pallas as pl
from jax.experimental.pallas import tpu as pltpu
from jax.sharding import PartitionSpec as P

EPS = 1e-06
INV_ROOT = 1.0 / math.sqrt(2.0)
BF16 = jnp.bfloat16
F32 = jnp.float32
ON_CHIP = pl.BlockSpec(memory_space=pltpu.VMEM)
SCALARS = pl.BlockSpec(memory_space=pltpu.SMEM)
ANYWHERE = pl.BlockSpec(memory_space=pl.ANY)
BLOCK_XOR = (0, 2, 1, 3)
AFTER_ATTEND = (4, 4)
AFTER_FEED = (3, 3, 2)
BEFORE_FEED = (3, 3, 2)
TILE = 256
FIRST_CUT = 1


def exchange(value, axis, flip):
    return lax.ppermute(value, axis, [(i, i ^ flip) for i in range(lax.axis_size(axis))])


def after(value, *earlier):
    return lax.optimization_barrier((value, *earlier))[0]


def normed(values, gain):
    scale = lax.rsqrt(jnp.mean(values * values, axis=-1, keepdims=True) + EPS)
    return values * scale * gain


def rotated(values, cos, sin):
    half = values.shape[-1] // 2
    first, second = values[:, :half], values[:, half:]
    return jnp.concatenate(
        [first * cos - second * sin, second * cos + first * sin], axis=-1
    )


def params(mib):
    return pltpu.CompilerParams(vmem_limit_bytes=mib << 20)


def cost(flops):
    return pl.CostEstimate(flops=int(flops), bytes_accessed=1, transcendentals=0)


def active_rows(hidden, gain):
    return normed(hidden.astype(F32), gain).astype(BF16)


def base_kernel(hidden_ref, gains_ref, left_ref, right_ref, out_ref):
    for r in range(hidden_ref.shape[0]):
        hidden = hidden_ref[r]
        active = active_rows(hidden, gains_ref[0:1, :])
        mid = lax.dot_general(
            active, left_ref[...], (((1,), (1,)), ((), ())), preferred_element_type=F32
        ).astype(BF16)
        low = jnp.dot(mid, right_ref[...], preferred_element_type=F32)
        out_ref[r] = hidden.astype(F32) + active.astype(F32) + normed(low, gains_ref[1:2, :])


def make_base(hidden, gains, left_t, right, flops=1):
    return pl.pallas_call(
        base_kernel,
        out_shape=jax.ShapeDtypeStruct(hidden.shape, F32),
        in_specs=[ON_CHIP] * 4,
        out_specs=ON_CHIP,
        cost_estimate=pl.CostEstimate(flops=int(flops), bytes_accessed=1, transcendentals=0),
        compiler_params=params(8),
        name="base",
    )(hidden, gains, left_t, right)


def active_kernel(hidden_ref, c_ref, gains_ref, own_ref, c_out_ref):
    for r in range(hidden_ref.shape[0]):
        own_ref[r] = active_rows(hidden_ref[r], gains_ref[0:1, :])
        c_out_ref[r] = active_rows(c_ref[r], gains_ref[0:1, :])


def make_active(hidden, c, gains):
    return pl.pallas_call(
        active_kernel,
        out_shape=[jax.ShapeDtypeStruct(hidden.shape, BF16)] * 2,
        in_specs=[ON_CHIP] * 3,
        out_specs=[ON_CHIP] * 2,
        cost_estimate=cost(1),
        compiler_params=params(4),
        name="active",
    )(hidden, c, gains)


def project_kernel(
    reqs,
    pages_in,
    len_ref,
    own_ref,
    y_ref,
    c_ref,
    d_ref,
    gains_ref,
    wq_ref,
    wkv_ref,
    head_gains_ref,
    cos_ref,
    sin_ref,
    *refs,
):
    page_ref, q_ref, quarter_ref = refs[pages_in:]
    member = lax.axis_index("mlp")
    part = own_ref.shape[1]
    head = head_gains_ref.shape[-1]
    qgain, kgain = head_gains_ref[0:1, :], head_gains_ref[1:2, :]
    starts = [pl.multiple_of((member ^ flip) * part, part) for flip in BLOCK_XOR]
    cos = jnp.concatenate([cos_ref[pl.ds(s, part), :] for s in starts], axis=0)
    sin = jnp.concatenate([sin_ref[pl.ds(s, part), :] for s in starts], axis=0)
    holds_keys = member % 2 == 0
    heads = wq_ref.shape[1] // head
    for i, r in enumerate(reqs):
        rows = jnp.concatenate(
            [
                own_ref[r],
                active_rows(y_ref[r], gains_ref[0:1, :]),
                c_ref[r],
                active_rows(d_ref[r], gains_ref[0:1, :]),
            ],
            axis=0,
        )
        count = rows.shape[0]
        raw = jnp.dot(rows, wkv_ref[...], preferred_element_type=F32)
        quarter = jnp.where(holds_keys, rotated(normed(raw, kgain), cos, sin), normed(raw, 1.0))
        quarter_ref[i] = quarter.astype(BF16)
        live = len_ref[r]
        for b, start in enumerate(starts):
            position = start + lax.broadcasted_iota(jnp.int32, (part, 1), 0)
            page_ref[i, pl.ds(start, part), :] = jnp.where(
                position < live, quarter[b * part : (b + 1) * part], 0.0
            ).astype(BF16)
        for h in range(heads):
            raw = jnp.dot(
                rows, wq_ref[:, h * head : (h + 1) * head], preferred_element_type=F32
            )
            q_ref[i, h * count : (h + 1) * count, :] = rotated(
                normed(raw, qgain), cos, sin
            ).astype(BF16)


def project(reqs, pages, lens, hidden, y, c, d, gains, wq, wkv, head_gains, cos, sin):
    part = hidden.shape[1]
    count = part * len(BLOCK_XOR)
    head = head_gains.shape[-1]
    heads = wq.shape[1] // head
    here = len(reqs)
    extra = [] if pages is None else [pages]
    return pl.pallas_call(
        functools.partial(project_kernel, reqs, len(extra)),
        grid=(1,),
        out_shape=[
            jax.ShapeDtypeStruct((hidden.shape[0], count, head), BF16),
            jax.ShapeDtypeStruct((here, heads * count, head), BF16),
            jax.ShapeDtypeStruct((here, count, head), BF16),
        ],
        in_specs=[SCALARS] + [ON_CHIP] * 10 + [ANYWHERE] * len(extra),
        out_specs=[
            pl.BlockSpec((here, count, head), lambda i: (reqs[0] // here, 0, 0)),
            ON_CHIP,
            ON_CHIP,
        ],
        input_output_aliases={11: 0} if extra else {},
        compiler_params=params(10),
        cost_estimate=cost(1),
        name="project",
    )(lens, hidden, y, c, d, gains, wq, wkv, head_gains, cos, sin, *extra)


def attend_kernel(
    req,
    index,
    offset,
    rows,
    sources,
    group_ref,
    owner_ref,
    slot_ref,
    q_ref,
    mine_ref,
    other_ref,
    wo_ref,
    *refs,
):
    pool_count = len({name for name, _, _, _ in sources})
    pool_refs = refs[:pool_count]
    outs = refs[pool_count:-4]
    keyval, mixed, place, sems = refs[-4:]
    member = lax.axis_index("mlp")
    me = lax.axis_index("req")
    count, head = mine_ref.shape[1:]
    part = count // len(BLOCK_XOR)
    page = pool_refs[0].shape[1]
    n_pages = owner_ref.shape[1]
    per_part = len(sources) // 2
    group = group_ref[req]
    for s in range(len(sources)):
        place[s] = -1
    for i in range(n_pages):
        flip = owner_ref[group, i] ^ me
        far = slot_ref[group, i] ^ (member % 2)
        place[far * per_part + flip] = i
    for name, entry, far, flip in sources:
        where = place[far * per_part + flip]

        @pl.when(where >= 0)
        def _():
            start = pl.multiple_of(where * page, page)
            pltpu.make_async_copy(
                pool_refs[name].at[entry], keyval.at[pl.ds(start, page), :], sems.at[where]
            ).start()

    pre = n_pages * page
    holds_keys = member % 2 == 0

    half = count // 2

    def place_suffix(mine_cols, other_cols):
        keyval[pre:, mine_cols] = mine_ref[index]
        keyval[pre : pre + half, other_cols] = other_ref[index, half:, :]
        keyval[pre + half :, other_cols] = other_ref[index, :half, :]

    @pl.when(holds_keys)
    def _():
        place_suffix(slice(0, head), slice(head, 2 * head))

    @pl.when(jnp.logical_not(holds_keys))
    def _():
        place_suffix(slice(head, 2 * head), slice(0, head))

    for i in range(n_pages):
        pltpu.make_async_copy(
            pool_refs[0].at[0], keyval.at[i * page : (i + 1) * page, :], sems.at[i]
        ).wait()

    factor = head**-0.5 * math.log2(math.e)
    column = lax.broadcasted_iota(jnp.int32, (1, count), 1)
    block = column // part
    key_at = (member ^ ((block & 1) * 2 + (block >> 1))) * part + column % part
    heads = q_ref.shape[1] // count
    pieces = [(h, b) for h in range(heads) for b in range(len(BLOCK_XOR))]
    per_step = max(1, TILE // rows)
    for first in range(0, len(pieces), per_step):
        step = pieces[first : first + per_step]
        starts = [h * count + b * part + offset for h, b in step]
        queries = jnp.concatenate([q_ref[index, s : s + rows, :] for s in starts], axis=0)
        query_at = jnp.concatenate(
            [
                (member ^ BLOCK_XOR[b]) * part
                + offset
                + lax.broadcasted_iota(jnp.int32, (rows, 1), 0)
                for _, b in step
            ],
            axis=0,
        )
        scores = lax.dot_general(
            queries,
            keyval[:, :head],
            (((1,), (1,)), ((), ())),
            preferred_element_type=F32,
        )
        scores = jnp.concatenate(
            [scores[:, :pre], jnp.where(key_at <= query_at, scores[:, pre:], -jnp.inf)], axis=1
        )
        peak = jnp.max(scores, axis=-1, keepdims=True)
        exps = jnp.exp2((scores - peak) * factor)
        total = jnp.sum(exps, axis=-1, keepdims=True)
        out = jnp.dot(exps.astype(BF16), keyval[:, head:], preferred_element_type=F32)
        out = (out * (1.0 / total)).astype(BF16)
        for i, (h, b) in enumerate(step):
            mixed[b * rows : (b + 1) * rows, h * head : (h + 1) * head] = out[
                i * rows : (i + 1) * rows
            ]
    width = wo_ref.shape[1]
    step = 512
    for col in range(0, width, step):
        result = jnp.dot(
            mixed[...], wo_ref[:, col : col + step], preferred_element_type=F32
        ).astype(BF16)
        store_rows(outs, col, result)


def store_rows(outs, col, result):
    first = 0
    for out_ref in outs:
        rows = out_ref.shape[0]
        out_ref[:, col : col + result.shape[1]] = result[first : first + rows]
        first += rows


def piece_shapes(part, width, pieces):
    return [jax.ShapeDtypeStruct((part // 4 * piece, width), BF16) for piece in pieces]


def partial_shapes(part, width, pieces):
    kept = jax.ShapeDtypeStruct((2 * part, width), BF16)
    return [kept] + piece_shapes(part, width, pieces)


def attend(req, index, offset, rows, sources, group, owner, slot, q, mine, other, wo, pools):
    count, head = mine.shape[1:]
    heads = q.shape[1] // count
    page = pools[0].shape[1]
    n_pages = owner.shape[1]
    keys = n_pages * page + count
    return pl.pallas_call(
        functools.partial(attend_kernel, req, index, offset, rows, sources),
        out_shape=partial_shapes(rows, wo.shape[1], AFTER_ATTEND),
        in_specs=[SCALARS] * 3 + [ON_CHIP] * 4 + [ANYWHERE] * len(pools),
        out_specs=[ON_CHIP] * (1 + len(AFTER_ATTEND)),
        scratch_shapes=[
            pltpu.VMEM((keys, 2 * head), BF16),
            pltpu.VMEM((len(BLOCK_XOR) * rows, heads * head), BF16),
            pltpu.SMEM((len(sources),), jnp.int32),
            pltpu.SemaphoreType.DMA((n_pages,)),
        ],
        compiler_params=params(8),
        cost_estimate=cost(1),
        name="attend",
    )(group, owner, slot, q, mine, other, wo, *pools)


def pair_kernel(count, keep_ref, *refs):
    others, outs = refs[:count], refs[count:]
    total = keep_ref[...].astype(F32) + jnp.concatenate(
        [ref[...].astype(F32) for ref in others], axis=0
    )
    store_rows(outs, 0, total.astype(BF16))


def pair_sum(keep, others, parts):
    rows, width = keep.shape
    return pl.pallas_call(
        functools.partial(pair_kernel, len(others)),
        out_shape=[jax.ShapeDtypeStruct((rows // parts, width), BF16)] * parts,
        in_specs=[ON_CHIP] * (1 + len(others)),
        out_specs=[ON_CHIP] * parts,
        cost_estimate=cost(1),
        compiler_params=params(6),
        name="pair_sum",
    )(keep, *others)


def residual_kernel(req, count, gains_ref, own_base_ref, y_base_ref, *refs):
    near_refs, far_refs = refs[:count], refs[count : 2 * count]
    res_ref, in_refs = refs[2 * count], refs[2 * count + 1 :]
    blocks = []
    for b, base_ref in enumerate((own_base_ref, y_base_ref)):
        sums = []
        for near_ref, far_ref in zip(near_refs, far_refs):
            rows = near_ref.shape[0] // 2
            mine = slice(b * rows, (b + 1) * rows)
            theirs = slice((1 - b) * rows, (2 - b) * rows)
            sums.append(near_ref[mine, :].astype(F32) + far_ref[theirs, :].astype(F32))
        total = jnp.concatenate(sums, axis=0)
        residual = (base_ref[req] + normed(total, gains_ref[2:3, :])) * INV_ROOT
        if b == 0:
            res_ref[...] = residual
        blocks.append(normed(residual, gains_ref[3:4, :]).astype(BF16))
    store_rows(in_refs, 0, jnp.concatenate(blocks, axis=0))


def make_residual(req, gains, own_base, y_base, near, far):
    part, width = own_base.shape[1:]
    return pl.pallas_call(
        functools.partial(residual_kernel, req, len(near)),
        out_shape=[jax.ShapeDtypeStruct((part, width), F32)]
        + piece_shapes(part, width, BEFORE_FEED),
        in_specs=[ON_CHIP] * (3 + 2 * len(near)),
        out_specs=[ON_CHIP] * (1 + len(BEFORE_FEED)),
        cost_estimate=cost(1e11),
        compiler_params=params(4),
        name="residual",
    )(gains, own_base, y_base, *near, *far)


def feed_kernel(count, gate_ref, up_ref, down_ref, *refs):
    outs, hidden = refs[count:-1], refs[-1]
    rows = jnp.concatenate([ref[...] for ref in refs[:count]], axis=0)
    units = gate_ref.shape[1]
    step = 512
    for u in range(0, units, step):
        gate = jnp.dot(rows, gate_ref[:, u : u + step], preferred_element_type=F32)
        up = jnp.dot(rows, up_ref[:, u : u + step], preferred_element_type=F32)
        hidden[:, u : u + step] = (jax.nn.gelu(gate, approximate=True) * up).astype(BF16)
    for col in range(0, down_ref.shape[1], step):
        result = jnp.dot(
            hidden[...], down_ref[:, col : col + step], preferred_element_type=F32
        ).astype(BF16)
        store_rows(outs, col, result)


def feed(pieces, gate, up, down):
    width, units = gate.shape
    part = sum(piece.shape[0] for piece in pieces) // 4
    return pl.pallas_call(
        functools.partial(feed_kernel, len(pieces)),
        out_shape=partial_shapes(part, width, AFTER_FEED),
        in_specs=[ON_CHIP] * (3 + len(pieces)),
        out_specs=[ON_CHIP] * (1 + len(AFTER_FEED)),
        scratch_shapes=[pltpu.VMEM((4 * part, units), BF16)],
        compiler_params=params(8),
        cost_estimate=cost(1),
        name="feed",
    )(gate, up, down, *pieces)


def finish_kernel(req, len_ref, res_ref, near_ref, far_ref, gains_ref, *refs):
    out_ref = refs[-1]
    part = res_ref.shape[0]
    total = near_ref[...].astype(F32) + far_ref[...].astype(F32)
    output = res_ref[...] + normed(total, gains_ref[4:5, :])
    position = lax.axis_index("mlp") * part + lax.broadcasted_iota(jnp.int32, (part, 1), 0)
    out_ref[0] = jnp.where(position < len_ref[req], output, 0.0).astype(BF16)


def finish(req, reqs, lens, residual, near, far, gains, before):
    part, width = residual.shape
    extra = [] if before is None else [before]
    return pl.pallas_call(
        functools.partial(finish_kernel, req),
        grid=(1,),
        out_shape=jax.ShapeDtypeStruct((reqs, part, width), BF16),
        in_specs=[SCALARS] + [ON_CHIP] * 4 + [ANYWHERE] * len(extra),
        out_specs=pl.BlockSpec((1, part, width), lambda i: (req, 0, 0)),
        input_output_aliases={5: 0} if extra else {},
        cost_estimate=cost(1e11 if req == 0 else 1),
        compiler_params=params(4),
        name="finish",
    )(lens, residual, near, far, gains, *extra)


def local(
    hidden_in,
    input_gain,
    query_weight,
    keyval_weight,
    query_gain,
    key_gain,
    out_weight,
    attn_gain,
    laurel_left,
    laurel_right,
    laurel_gain,
    ffn_gain,
    post_gain,
    gate_projection_matrix,
    up_projection_matrix,
    down_projection_matrix,
    page_pool,
    page_owner,
    page_slot,
    request_group,
    suffix_len,
):
    member = lax.axis_index("mlp")
    part, reqs, width = hidden_in.shape
    head = query_gain.shape[0]
    count = part * lax.axis_size("mlp")
    prefix_len = page_owner.shape[1] * page_pool.shape[1]

    hidden = jnp.transpose(hidden_in, (1, 0, 2))
    gains = jnp.stack([input_gain, laurel_gain, attn_gain, ffn_gain, post_gain])
    head_gains = jnp.stack([query_gain, key_gain])
    half = head // 2
    frequency = 1000000.0 ** (-jnp.arange(half, dtype=F32) / half)
    angles = (prefix_len + jnp.arange(count)).astype(F32)[:, None] * frequency[None, :]
    cos, sin = jnp.cos(angles), jnp.sin(angles)

    hidden_y = exchange(hidden, "mlp", 2)
    hidden_c = exchange(hidden, "mlp", 1)

    page_rows = page_pool.shape[1]
    own_page = lax.dynamic_slice(
        after(page_pool, hidden_c), (member % 2, 0, member // 2 * 2 * head), (1, page_rows, 2 * head)
    )
    later = list(range(4, lax.axis_size("req"), 2))
    direct = {flip: exchange(own_page, "req", flip) for flip in [*later, 2]}
    near_pages = jnp.concatenate([own_page, after(direct[2], cos, gains, head_gains)])
    near_odd = exchange(near_pages, "req", 1)
    own_base = make_base(after(hidden, near_pages), gains, laurel_left.T, laurel_right)
    far_pages = [direct[flip] for flip in later]
    own_active, c_active = make_active(after(hidden, own_base), hidden_c, gains)
    far_pages[0] = after(far_pages[0], own_active)
    far_pages = jnp.concatenate(far_pages)
    far_odd = exchange(far_pages, "req", 1)
    far_other = exchange(far_pages, "mlp", 1)
    near_other = exchange(near_pages, "mlp", 1)
    hidden_y = after(hidden_y, far_pages)
    hidden_d = exchange(hidden_y, "mlp", 1)
    y_base = make_base(hidden_y, gains, laurel_left.T, laurel_right, 1e11)
    hidden_y = after(hidden_y, y_base)

    def project_some(some, pages, *earlier):
        return project(
            some,
            pages,
            suffix_len,
            after(own_active, *earlier),
            hidden_y,
            c_active,
            hidden_d,
            gains,
            query_weight,
            keyval_weight,
            head_gains,
            cos,
            sin,
        )

    pages, q_first, kv_first = project_some([0], None)
    projected = [(q_first, kv_first, exchange(kv_first, "mlp", 1), 0)]
    near_odd = after(near_odd, q_first)
    near_odd_other = exchange(near_odd, "mlp", 1)
    far_odd = after(far_odd, q_first)
    far_odd_other = exchange(far_odd, "mlp", 1)
    pools = [near_pages, far_pages, near_odd, far_odd]
    pools += [near_other, far_other, near_odd_other, far_odd_other]
    flips = [[0, 2], later, [1, 3], [flip + 1 for flip in later]]
    sources = [
        (p, i, p // 4, flip) for p in range(len(pools)) for i, flip in enumerate(flips[p % 4])
    ]

    pages, q_next, kv_next = project_some([1], pages, q_first)
    projected.append((q_next, kv_next, exchange(kv_next, "mlp", 1), 0))

    def attend_one(r, offset, rows, *earlier):
        q, mine, other, index = projected[r]
        return attend(
            r,
            index,
            offset,
            rows,
            sources,
            request_group,
            page_owner,
            page_slot,
            after(q, *earlier),
            mine,
            other,
            out_weight,
            pools,
        )

    def swap(pieces):
        return [exchange(piece, "mlp", 1) for piece in pieces]

    def residual_one(r, *earlier):
        first, *rest = far[r]
        residual, *pieces = make_residual(
            r, gains, own_base, y_base, near[r], [after(first, *earlier), *rest]
        )
        residuals[r] = residual
        inputs[r] = pieces + swap(pieces)
        return pieces[0]

    def feed_one(r, *earlier):
        first, *rest = inputs[r]
        return feed(
            [after(first, *earlier), *rest],
            gate_projection_matrix,
            up_projection_matrix,
            down_projection_matrix,
        )

    def finish_one(r, earlier, before):
        near_own, far_own = done[r]
        return finish(
            r,
            reqs,
            suffix_len,
            residuals[r],
            near_own,
            after(far_own, earlier),
            gains,
            before,
        )

    near, far, residuals, inputs = {}, {}, {}, {}
    last = q_next
    for r in range(reqs):
        rows = part // FIRST_CUT if r == 0 else part
        near[r], far[r] = [], []
        for offset in range(0, part, rows):
            keep, *pieces = attend_one(r, offset, rows, last)
            others = swap(pieces)
            last = keep
            if r >= 2:
                last = residual_one(r - 2, last)
            (joined,) = pair_sum(after(keep, last), others, 1)
            near[r].append(joined)
            far[r].append(exchange(joined, "mlp", 2))
            last = joined
        if r + 2 < reqs:
            pages, q_next, kv_next = project_some([r + 2], pages, last)
            projected.append((q_next, kv_next, exchange(kv_next, "mlp", 1), 0))
            last = q_next
    done, result = {}, None
    for r in range(reqs):
        keep, *pieces = feed_one(r, last)
        others = swap(pieces)
        last = keep
        if r + 1 < reqs:
            last = residual_one(r + 1, last)
        else:
            last = result = finish_one(0, last, None)
        near_own, near_y = pair_sum(after(keep, last), others, 2)
        done[r] = (near_own, exchange(near_y, "mlp", 2))
        last = near_own
    for r in range(1, reqs):
        result = finish_one(r, last, result)
    return jnp.transpose(result, (1, 0, 2)), jnp.transpose(pages, (1, 0, 2))


def solution(mesh):
    placed = (
        P("mlp", "req", None),
        P(),
        P(None, "mlp"),
        P(None, "mlp"),
        P(),
        P(),
        P("mlp", None),
        P(),
        P(),
        P(),
        P(),
        P(),
        P(),
        P(None, "mlp"),
        P(None, "mlp"),
        P("mlp", None),
        P("req", None, None),
        P(),
        P(),
        P("req"),
        P("req"),
    )
    return jax.shard_map(
        local,
        mesh=mesh,
        in_specs=placed,
        out_specs=(P("mlp", "req", None), P(None, "req", "mlp")),
        check_vma=False,
    )
```

```python
import functools
import math

import jax
import jax.numpy as jnp
from jax import lax
from jax.experimental import pallas as pl
from jax.experimental.pallas import tpu as pltpu
from jax.sharding import PartitionSpec as P

EPS = 1e-06
INV_ROOT = 1.0 / math.sqrt(2.0)
BF16 = jnp.bfloat16
F32 = jnp.float32
ON_CHIP = pl.BlockSpec(memory_space=pltpu.VMEM)
SCALARS = pl.BlockSpec(memory_space=pltpu.SMEM)
ANYWHERE = pl.BlockSpec(memory_space=pl.ANY)
BLOCK_XOR = (0, 2, 1, 3)
AFTER_FIRST_ATTEND = (8,)
AFTER_ATTEND = (4, 4)
AFTER_FEED = (3, 3, 2)
BEFORE_FEED = (3, 3, 2)
TILE = 256
FIRST_CUT = 1


def exchange(value, axis, flip):
    return lax.ppermute(value, axis, [(i, i ^ flip) for i in range(lax.axis_size(axis))])


def after(value, *earlier):
    return lax.optimization_barrier((value, *earlier))[0]


def normed(values, gain):
    scale = lax.rsqrt(jnp.mean(values * values, axis=-1, keepdims=True) + EPS)
    return values * scale * gain


def rotated(values, cos, sin):
    half = values.shape[-1] // 2
    first, second = values[:, :half], values[:, half:]
    return jnp.concatenate(
        [first * cos - second * sin, second * cos + first * sin], axis=-1
    )


def params(mib):
    return pltpu.CompilerParams(vmem_limit_bytes=mib << 20)


def cost(flops):
    return pl.CostEstimate(flops=int(flops), bytes_accessed=1, transcendentals=0)


def active_rows(hidden, gain):
    return normed(hidden.astype(F32), gain).astype(BF16)


def base_kernel(hidden_ref, gains_ref, left_ref, right_ref, out_ref):
    for r in range(hidden_ref.shape[0]):
        hidden = hidden_ref[r]
        active = active_rows(hidden, gains_ref[0:1, :])
        mid = lax.dot_general(
            active, left_ref[...], (((1,), (1,)), ((), ())), preferred_element_type=F32
        ).astype(BF16)
        low = jnp.dot(mid, right_ref[...], preferred_element_type=F32)
        out_ref[r] = hidden.astype(F32) + active.astype(F32) + normed(low, gains_ref[1:2, :])


def make_base(hidden, gains, left_t, right, flops=1):
    return pl.pallas_call(
        base_kernel,
        out_shape=jax.ShapeDtypeStruct(hidden.shape, F32),
        in_specs=[ON_CHIP] * 4,
        out_specs=ON_CHIP,
        cost_estimate=pl.CostEstimate(flops=int(flops), bytes_accessed=1, transcendentals=0),
        compiler_params=params(8),
        name="base",
    )(hidden, gains, left_t, right)


def project_kernel(
    reqs,
    pages_in,
    len_ref,
    hidden_ref,
    y_ref,
    c_ref,
    d_ref,
    gains_ref,
    wq_ref,
    wkv_ref,
    head_gains_ref,
    cos_ref,
    sin_ref,
    *refs,
):
    page_ref, q_ref, quarter_ref = refs[pages_in:]
    member = lax.axis_index("mlp")
    part = hidden_ref.shape[1]
    head = head_gains_ref.shape[-1]
    qgain, kgain = head_gains_ref[0:1, :], head_gains_ref[1:2, :]
    starts = [pl.multiple_of((member ^ flip) * part, part) for flip in BLOCK_XOR]
    cos = jnp.concatenate([cos_ref[pl.ds(s, part), :] for s in starts], axis=0)
    sin = jnp.concatenate([sin_ref[pl.ds(s, part), :] for s in starts], axis=0)
    holds_keys = member % 2 == 0
    heads = wq_ref.shape[1] // head
    for i, r in enumerate(reqs):
        rows = jnp.concatenate(
            [
                active_rows(ref[r], gains_ref[0:1, :])
                for ref in (hidden_ref, y_ref, c_ref, d_ref)
            ],
            axis=0,
        )
        count = rows.shape[0]
        raw = jnp.dot(rows, wkv_ref[...], preferred_element_type=F32)
        quarter = jnp.where(holds_keys, rotated(normed(raw, kgain), cos, sin), normed(raw, 1.0))
        quarter_ref[i] = quarter.astype(BF16)
        live = len_ref[r]
        for b, start in enumerate(starts):
            position = start + lax.broadcasted_iota(jnp.int32, (part, 1), 0)
            page_ref[i, pl.ds(start, part), :] = jnp.where(
                position < live, quarter[b * part : (b + 1) * part], 0.0
            ).astype(BF16)
        for h in range(heads):
            raw = jnp.dot(
                rows, wq_ref[:, h * head : (h + 1) * head], preferred_element_type=F32
            )
            q_ref[i, h * count : (h + 1) * count, :] = rotated(
                normed(raw, qgain), cos, sin
            ).astype(BF16)


def project(reqs, pages, lens, hidden, y, c, d, gains, wq, wkv, head_gains, cos, sin):
    part = hidden.shape[1]
    count = part * len(BLOCK_XOR)
    head = head_gains.shape[-1]
    heads = wq.shape[1] // head
    here = len(reqs)
    extra = [] if pages is None else [pages]
    return pl.pallas_call(
        functools.partial(project_kernel, reqs, len(extra)),
        grid=(1,),
        out_shape=[
            jax.ShapeDtypeStruct((hidden.shape[0], count, head), BF16),
            jax.ShapeDtypeStruct((here, heads * count, head), BF16),
            jax.ShapeDtypeStruct((here, count, head), BF16),
        ],
        in_specs=[SCALARS] + [ON_CHIP] * 10 + [ANYWHERE] * len(extra),
        out_specs=[
            pl.BlockSpec((here, count, head), lambda i: (reqs[0] // here, 0, 0)),
            ON_CHIP,
            ON_CHIP,
        ],
        input_output_aliases={11: 0} if extra else {},
        compiler_params=params(10),
        cost_estimate=cost(1),
        name="project",
    )(lens, hidden, y, c, d, gains, wq, wkv, head_gains, cos, sin, *extra)


def attend_kernel(
    req,
    index,
    offset,
    rows,
    sources,
    group_ref,
    owner_ref,
    slot_ref,
    q_ref,
    mine_ref,
    other_ref,
    wo_ref,
    *refs,
):
    pool_count = len({name for name, _, _, _ in sources})
    pool_refs = refs[:pool_count]
    outs = refs[pool_count:-4]
    keyval, mixed, place, sems = refs[-4:]
    member = lax.axis_index("mlp")
    me = lax.axis_index("req")
    count, head = mine_ref.shape[1:]
    part = count // len(BLOCK_XOR)
    page = pool_refs[0].shape[1]
    n_pages = owner_ref.shape[1]
    per_part = len(sources) // 2
    group = group_ref[req]
    for s in range(len(sources)):
        place[s] = -1
    for i in range(n_pages):
        flip = owner_ref[group, i] ^ me
        far = slot_ref[group, i] ^ (member % 2)
        place[far * per_part + flip] = i
    for name, entry, far, flip in sources:
        where = place[far * per_part + flip]

        @pl.when(where >= 0)
        def _():
            start = pl.multiple_of(where * page, page)
            pltpu.make_async_copy(
                pool_refs[name].at[entry], keyval.at[pl.ds(start, page), :], sems.at[where]
            ).start()

    pre = n_pages * page
    holds_keys = member % 2 == 0

    half = count // 2

    def place_suffix(mine_cols, other_cols):
        keyval[pre:, mine_cols] = mine_ref[index]
        keyval[pre : pre + half, other_cols] = other_ref[index, half:, :]
        keyval[pre + half :, other_cols] = other_ref[index, :half, :]

    @pl.when(holds_keys)
    def _():
        place_suffix(slice(0, head), slice(head, 2 * head))

    @pl.when(jnp.logical_not(holds_keys))
    def _():
        place_suffix(slice(head, 2 * head), slice(0, head))

    for i in range(n_pages):
        pltpu.make_async_copy(
            pool_refs[0].at[0], keyval.at[i * page : (i + 1) * page, :], sems.at[i]
        ).wait()

    factor = head**-0.5 * math.log2(math.e)
    column = lax.broadcasted_iota(jnp.int32, (1, count), 1)
    block = column // part
    key_at = (member ^ ((block & 1) * 2 + (block >> 1))) * part + column % part
    heads = q_ref.shape[1] // count
    pieces = [(h, b) for h in range(heads) for b in range(len(BLOCK_XOR))]
    per_step = max(1, TILE // rows)
    for first in range(0, len(pieces), per_step):
        step = pieces[first : first + per_step]
        starts = [h * count + b * part + offset for h, b in step]
        queries = jnp.concatenate([q_ref[index, s : s + rows, :] for s in starts], axis=0)
        query_at = jnp.concatenate(
            [
                (member ^ BLOCK_XOR[b]) * part
                + offset
                + lax.broadcasted_iota(jnp.int32, (rows, 1), 0)
                for _, b in step
            ],
            axis=0,
        )
        scores = lax.dot_general(
            queries,
            keyval[:, :head],
            (((1,), (1,)), ((), ())),
            preferred_element_type=F32,
        )
        scores = jnp.concatenate(
            [scores[:, :pre], jnp.where(key_at <= query_at, scores[:, pre:], -jnp.inf)], axis=1
        )
        peak = jnp.max(scores, axis=-1, keepdims=True)
        exps = jnp.exp2((scores - peak) * factor)
        total = jnp.sum(exps, axis=-1, keepdims=True)
        out = jnp.dot(exps.astype(BF16), keyval[:, head:], preferred_element_type=F32)
        out = (out * (1.0 / total)).astype(BF16)
        for i, (h, b) in enumerate(step):
            mixed[b * rows : (b + 1) * rows, h * head : (h + 1) * head] = out[
                i * rows : (i + 1) * rows
            ]
    width = wo_ref.shape[1]
    step = 512
    for col in range(0, width, step):
        result = jnp.dot(
            mixed[...], wo_ref[:, col : col + step], preferred_element_type=F32
        ).astype(BF16)
        store_rows(outs, col, result)


def store_rows(outs, col, result):
    first = 0
    for out_ref in outs:
        rows = out_ref.shape[0]
        out_ref[:, col : col + result.shape[1]] = result[first : first + rows]
        first += rows


def piece_shapes(part, width, pieces):
    return [jax.ShapeDtypeStruct((part // 4 * piece, width), BF16) for piece in pieces]


def partial_shapes(part, width, pieces):
    kept = jax.ShapeDtypeStruct((2 * part, width), BF16)
    return [kept] + piece_shapes(part, width, pieces)


def attend(req, index, offset, rows, sources, group, owner, slot, q, mine, other, wo, pools):
    pieces = AFTER_ATTEND if req else AFTER_FIRST_ATTEND
    count, head = mine.shape[1:]
    heads = q.shape[1] // count
    page = pools[0].shape[1]
    n_pages = owner.shape[1]
    keys = n_pages * page + count
    return pl.pallas_call(
        functools.partial(attend_kernel, req, index, offset, rows, sources),
        out_shape=partial_shapes(rows, wo.shape[1], pieces),
        in_specs=[SCALARS] * 3 + [ON_CHIP] * 4 + [ANYWHERE] * len(pools),
        out_specs=[ON_CHIP] * (1 + len(pieces)),
        scratch_shapes=[
            pltpu.VMEM((keys, 2 * head), BF16),
            pltpu.VMEM((len(BLOCK_XOR) * rows, heads * head), BF16),
            pltpu.SMEM((len(sources),), jnp.int32),
            pltpu.SemaphoreType.DMA((n_pages,)),
        ],
        compiler_params=params(8),
        cost_estimate=cost(1),
        name="attend",
    )(group, owner, slot, q, mine, other, wo, *pools)


def pair_kernel(count, keep_ref, *refs):
    others, outs = refs[:count], refs[count:]
    total = keep_ref[...].astype(F32) + jnp.concatenate(
        [ref[...].astype(F32) for ref in others], axis=0
    )
    store_rows(outs, 0, total.astype(BF16))


def pair_sum(keep, others, parts):
    rows, width = keep.shape
    return pl.pallas_call(
        functools.partial(pair_kernel, len(others)),
        out_shape=[jax.ShapeDtypeStruct((rows // parts, width), BF16)] * parts,
        in_specs=[ON_CHIP] * (1 + len(others)),
        out_specs=[ON_CHIP] * parts,
        cost_estimate=cost(1),
        compiler_params=params(6),
        name="pair_sum",
    )(keep, *others)


def residual_kernel(req, count, gains_ref, own_base_ref, y_base_ref, *refs):
    near_refs, far_refs = refs[:count], refs[count : 2 * count]
    res_ref, in_refs = refs[2 * count], refs[2 * count + 1 :]
    blocks = []
    for b, base_ref in enumerate((own_base_ref, y_base_ref)):
        sums = []
        for near_ref, far_ref in zip(near_refs, far_refs):
            rows = near_ref.shape[0] // 2
            mine = slice(b * rows, (b + 1) * rows)
            theirs = slice((1 - b) * rows, (2 - b) * rows)
            sums.append(near_ref[mine, :].astype(F32) + far_ref[theirs, :].astype(F32))
        total = jnp.concatenate(sums, axis=0)
        residual = (base_ref[req] + normed(total, gains_ref[2:3, :])) * INV_ROOT
        if b == 0:
            res_ref[...] = residual
        blocks.append(normed(residual, gains_ref[3:4, :]).astype(BF16))
    store_rows(in_refs, 0, jnp.concatenate(blocks, axis=0))


def make_residual(req, gains, own_base, y_base, near, far):
    part, width = own_base.shape[1:]
    return pl.pallas_call(
        functools.partial(residual_kernel, req, len(near)),
        out_shape=[jax.ShapeDtypeStruct((part, width), F32)]
        + piece_shapes(part, width, BEFORE_FEED),
        in_specs=[ON_CHIP] * (3 + 2 * len(near)),
        out_specs=[ON_CHIP] * (1 + len(BEFORE_FEED)),
        cost_estimate=cost(1e11),
        compiler_params=params(4),
        name="residual",
    )(gains, own_base, y_base, *near, *far)


def feed_kernel(count, gate_ref, up_ref, down_ref, *refs):
    outs, hidden = refs[count:-1], refs[-1]
    rows = jnp.concatenate([ref[...] for ref in refs[:count]], axis=0)
    units = gate_ref.shape[1]
    step = 512
    for u in range(0, units, step):
        gate = jnp.dot(rows, gate_ref[:, u : u + step], preferred_element_type=F32)
        up = jnp.dot(rows, up_ref[:, u : u + step], preferred_element_type=F32)
        hidden[:, u : u + step] = (jax.nn.gelu(gate, approximate=True) * up).astype(BF16)
    for col in range(0, down_ref.shape[1], step):
        result = jnp.dot(
            hidden[...], down_ref[:, col : col + step], preferred_element_type=F32
        ).astype(BF16)
        store_rows(outs, col, result)


def feed(pieces, gate, up, down):
    width, units = gate.shape
    part = sum(piece.shape[0] for piece in pieces) // 4
    return pl.pallas_call(
        functools.partial(feed_kernel, len(pieces)),
        out_shape=partial_shapes(part, width, AFTER_FEED),
        in_specs=[ON_CHIP] * (3 + len(pieces)),
        out_specs=[ON_CHIP] * (1 + len(AFTER_FEED)),
        scratch_shapes=[pltpu.VMEM((4 * part, units), BF16)],
        compiler_params=params(8),
        cost_estimate=cost(1),
        name="feed",
    )(gate, up, down, *pieces)


def finish_kernel(req, len_ref, res_ref, near_ref, far_ref, gains_ref, *refs):
    out_ref, rows_ref, sems = refs[-3:]
    part = res_ref.shape[0]
    steps = sems.shape[0]
    rows = part // steps
    copies = []
    for i in range(steps):
        here = slice(i * rows, (i + 1) * rows)
        total = near_ref[here, :].astype(F32) + far_ref[here, :].astype(F32)
        output = res_ref[here, :] + normed(total, gains_ref[4:5, :])
        position = (
            lax.axis_index("mlp") * part
            + i * rows
            + lax.broadcasted_iota(jnp.int32, (rows, 1), 0)
        )
        rows_ref[here, :] = jnp.where(position < len_ref[req], output, 0.0).astype(BF16)
        copies.append(
            pltpu.make_async_copy(rows_ref.at[here, :], out_ref.at[req, here, :], sems.at[i])
        )
        copies[-1].start()
    for copy in copies:
        copy.wait()


def finish(req, reqs, lens, residual, near, far, gains, before):
    part, width = residual.shape
    extra = [] if before is None else [before]
    return pl.pallas_call(
        functools.partial(finish_kernel, req),
        out_shape=jax.ShapeDtypeStruct((reqs, part, width), BF16),
        in_specs=[SCALARS] + [ON_CHIP] * 4 + [ANYWHERE] * len(extra),
        out_specs=ANYWHERE,
        input_output_aliases={5: 0} if extra else {},
        scratch_shapes=[pltpu.VMEM((part, width), BF16), pltpu.SemaphoreType.DMA((4,))],
        cost_estimate=cost(1e11 if req == 0 else 1),
        compiler_params=params(4),
        name="finish",
    )(lens, residual, near, far, gains, *extra)


def local(
    hidden_in,
    input_gain,
    query_weight,
    keyval_weight,
    query_gain,
    key_gain,
    out_weight,
    attn_gain,
    laurel_left,
    laurel_right,
    laurel_gain,
    ffn_gain,
    post_gain,
    gate_projection_matrix,
    up_projection_matrix,
    down_projection_matrix,
    page_pool,
    page_owner,
    page_slot,
    request_group,
    suffix_len,
):
    member = lax.axis_index("mlp")
    part, reqs, width = hidden_in.shape
    head = query_gain.shape[0]
    count = part * lax.axis_size("mlp")
    prefix_len = page_owner.shape[1] * page_pool.shape[1]

    hidden = jnp.transpose(hidden_in, (1, 0, 2))
    gains = jnp.stack([input_gain, laurel_gain, attn_gain, ffn_gain, post_gain])
    head_gains = jnp.stack([query_gain, key_gain])
    half = head // 2
    frequency = 1000000.0 ** (-jnp.arange(half, dtype=F32) / half)
    angles = (prefix_len + jnp.arange(count)).astype(F32)[:, None] * frequency[None, :]
    cos, sin = jnp.cos(angles), jnp.sin(angles)

    hidden_y = exchange(hidden, "mlp", 2)
    hidden_c = exchange(hidden, "mlp", 1)

    page_rows = page_pool.shape[1]
    own_page = lax.dynamic_slice(
        after(page_pool, hidden_c), (member % 2, 0, member // 2 * 2 * head), (1, page_rows, 2 * head)
    )
    later = list(range(4, lax.axis_size("req"), 2))
    direct = {flip: exchange(own_page, "req", flip) for flip in [*later, 2]}
    near_pages = jnp.concatenate([own_page, after(direct[2], cos, gains, head_gains)])
    near_odd = exchange(near_pages, "req", 1)
    own_base = make_base(after(hidden, near_pages), gains, laurel_left.T, laurel_right)
    far_pages = [direct[flip] for flip in later]
    far_pages[0] = after(far_pages[0], own_base)
    far_pages = jnp.concatenate(far_pages)
    far_odd = exchange(far_pages, "req", 1)
    far_other = exchange(far_pages, "mlp", 1)
    near_other = exchange(near_pages, "mlp", 1)
    hidden_y = after(hidden_y, far_pages)
    hidden_d = exchange(hidden_y, "mlp", 1)
    y_base = make_base(hidden_y, gains, laurel_left.T, laurel_right, 1e11)
    hidden_y = after(hidden_y, y_base)

    def project_some(some, pages, *earlier):
        return project(
            some,
            pages,
            suffix_len,
            after(hidden, *earlier),
            hidden_y,
            hidden_c,
            hidden_d,
            gains,
            query_weight,
            keyval_weight,
            head_gains,
            cos,
            sin,
        )

    pages, q_first, kv_first = project_some([0], None)
    projected = [(q_first, kv_first, exchange(kv_first, "mlp", 1), 0)]
    near_odd = after(near_odd, q_first)
    near_odd_other = exchange(near_odd, "mlp", 1)
    far_odd = after(far_odd, q_first)
    far_odd_other = exchange(far_odd, "mlp", 1)
    pools = [near_pages, far_pages, near_odd, far_odd]
    pools += [near_other, far_other, near_odd_other, far_odd_other]
    flips = [[0, 2], later, [1, 3], [flip + 1 for flip in later]]
    sources = [
        (p, i, p // 4, flip) for p in range(len(pools)) for i, flip in enumerate(flips[p % 4])
    ]

    pages, q_next, kv_next = project_some([1], pages, q_first)
    projected.append((q_next, kv_next, exchange(kv_next, "mlp", 1), 0))

    def attend_one(r, offset, rows, *earlier):
        q, mine, other, index = projected[r]
        return attend(
            r,
            index,
            offset,
            rows,
            sources,
            request_group,
            page_owner,
            page_slot,
            after(q, *earlier),
            mine,
            other,
            out_weight,
            pools,
        )

    def swap(pieces):
        return [exchange(piece, "mlp", 1) for piece in pieces]

    def residual_one(r, *earlier):
        first, *rest = far[r]
        residual, *pieces = make_residual(
            r, gains, own_base, y_base, near[r], [after(first, *earlier), *rest]
        )
        residuals[r] = residual
        inputs[r] = pieces + swap(pieces)
        return pieces[0]

    def feed_one(r, *earlier):
        first, *rest = inputs[r]
        return feed(
            [after(first, *earlier), *rest],
            gate_projection_matrix,
            up_projection_matrix,
            down_projection_matrix,
        )

    def finish_one(r, earlier, before):
        near_own, far_own = done[r]
        return finish(
            r,
            reqs,
            suffix_len,
            residuals[r],
            near_own,
            after(far_own, earlier),
            gains,
            before,
        )

    near, far, residuals, inputs = {}, {}, {}, {}
    last = q_next
    for r in range(reqs):
        rows = part // FIRST_CUT if r == 0 else part
        near[r], far[r] = [], []
        for offset in range(0, part, rows):
            keep, *pieces = attend_one(r, offset, rows, last)
            others = swap(pieces)
            last = keep
            if r >= 2:
                last = residual_one(r - 2, last)
            (joined,) = pair_sum(after(keep, last), others, 1)
            near[r].append(joined)
            far[r].append(exchange(joined, "mlp", 2))
            last = joined
        if r + 2 < reqs:
            pages, q_next, kv_next = project_some([r + 2], pages, last)
            projected.append((q_next, kv_next, exchange(kv_next, "mlp", 1), 0))
            last = q_next
    done, result = {}, None
    for r in range(reqs):
        keep, *pieces = feed_one(r, last)
        others = swap(pieces)
        last = keep
        if r + 1 < reqs:
            last = residual_one(r + 1, last)
        else:
            last = result = finish_one(0, last, None)
        near_own, near_y = pair_sum(after(keep, last), others, 2)
        done[r] = (near_own, exchange(near_y, "mlp", 2))
        last = near_own
    for r in range(1, reqs):
        result = finish_one(r, last, result)
    return jnp.transpose(result, (1, 0, 2)), jnp.transpose(pages, (1, 0, 2))


def solution(mesh):
    placed = (
        P("mlp", "req", None),
        P(),
        P(None, "mlp"),
        P(None, "mlp"),
        P(),
        P(),
        P("mlp", None),
        P(),
        P(),
        P(),
        P(),
        P(),
        P(),
        P(None, "mlp"),
        P(None, "mlp"),
        P("mlp", None),
        P("req", None, None),
        P(),
        P(),
        P("req"),
        P("req"),
    )
    return jax.shard_map(
        local,
        mesh=mesh,
        in_specs=placed,
        out_specs=(P("mlp", "req", None), P(None, "req", "mlp")),
        check_vma=False,
    )
```
